32 devices in a mesh: tm: 16 (over z, x, core), space: 2 (over y).
Axes of the slice: x: 2, y: 2, z: 4, core: 2. Of those that a mesh axis runs over, the one named last changes fastest.
Arguments:
- initial: float32 [16, 64, 128], P('space'), may hold values from -6 to 6
- forcing: bfloat16 [64, 16, 64, 128], P('tm', 'space'), may hold values from -4 to 4
- brick_blocks: bfloat16 [16, 64, 448], P('space'), may hold values from -1 to 1
- neighbours: int32 [16, 6], P('space'), may hold values from 0 to 15, as said below
- coarse_modes: float32 [8, 64], replicated, may hold values from -0.75 to 0.75
- coarse_blocks: float32 [16, 8, 8], P('space'), may hold values from -1 to 1.2
Outputs:
- solution: float32 [64, 16, 64, 128], P('tm', 'space')
- last_defect: float32 [16, 16, 64, 128], P('tm', 'space')
The draws below stay inside these ranges and needn't reach their ends.
Inputs may be any that keep to these rules, and one draw needn't show every extreme that they name: `neighbours`: each brick's 6 slots name distinct bricks other than itself, in a random slot order, each at most 4 positions away along the periodic brick order; every brick names the bricks directly before and after it and one brick exactly 4 away.
All inputs are finite; a program needn't handle non-finite values.
Results may differ from the reference program's by a relative error of at most 0.014.
Values may be sent and summed in bfloat16 or wider, within the bound.
No kernel may reach another device: no remote copies, remote signals or barrier semaphores. Data moves between devices by JAX's collectives and lax.ppermute only.
A program may use at most 64 MiB of HBM per device.

```python
import jax
import jax.numpy as jnp
from jax import lax

BRICK = 64
ENS = 128
NB = 6
REACH = 4
Q = 8
SWEEPS = 3
STEPS = 4
ITERS = 2
BRICKS = 16
NT = 64
N_TM = 16


def draw_brick_blocks(key, part):
    first_key = jax.random.fold_in(jax.random.fold_in(key, 11), 0)
    block_shape = (BRICKS, BRICK, (NB + 1) * BRICK)
    random_part = jnp.clip(jax.random.normal(first_key, block_shape, jnp.float32), -6.0, 6.0)
    spread = jnp.ones((BRICKS, 1, 1), jnp.float32)
    row_ids = jnp.arange(BRICK)[:, None]
    col_ids = jnp.arange((NB + 1) * BRICK)[None, :]
    leading = col_ids < BRICK
    entry_scale = jnp.where(leading, 0.25, 0.15 * spread) / jnp.sqrt(jnp.float32(BRICK))
    identity = (row_ids == col_ids).astype(jnp.float32)
    return (0.7 * identity + entry_scale * random_part).astype(jnp.bfloat16)


def draw_neighbours(key, part):
    sign_key, pick_key, order_key = jax.random.split(jax.random.fold_in(key, 37), 3)
    direction = 2 * jax.random.randint(sign_key, (BRICKS, 1), 0, 2) - 1
    middle = jnp.arange(2, REACH, dtype=jnp.int32)
    both_sides = jnp.concatenate([middle, -middle])[None, :]
    candidates = jnp.concatenate([jnp.broadcast_to(both_sides, (BRICKS, 2 * REACH - 4)), -direction * REACH], 1)
    pool_size = 2 * REACH - 3
    scores = jax.random.randint(pick_key, (BRICKS, pool_size), 0, 1 << 20) * pool_size + jnp.arange(pool_size, dtype=jnp.int32)
    chosen = jnp.take_along_axis(candidates, jnp.argsort(scores, axis=1)[:, :NB - 3], 1)
    fixed_part = jnp.concatenate([-jnp.ones((BRICKS, 1), jnp.int32), jnp.ones((BRICKS, 1), jnp.int32), direction * REACH], 1)
    offsets = jnp.concatenate([fixed_part, chosen], 1)
    order_scores = jax.random.randint(order_key, (BRICKS, NB), 0, 1 << 20) * NB + jnp.arange(NB, dtype=jnp.int32)
    offsets = jnp.take_along_axis(offsets, jnp.argsort(order_scores, axis=1), 1)
    return jnp.mod(jnp.arange(BRICKS, dtype=jnp.int32)[:, None] + offsets, BRICKS).astype(jnp.int32)


def draw_coarse_blocks(key, part):
    first_key, second_key = jax.random.split(jax.random.fold_in(key, 23))
    chain_length = NT // STEPS
    horizon = jnp.exp(jax.random.uniform(first_key, (BRICKS, Q), jnp.float32, jnp.log(0.25), jnp.log(8.0)))
    random_part = jnp.clip(jax.random.normal(second_key, (BRICKS, Q, Q), jnp.float32), -3.0, 3.0)
    decay_rates = jnp.power(0.1, horizon / chain_length)
    identity = jnp.eye(Q, dtype=jnp.float32)
    return decay_rates[:, :, None] * identity + 0.1 / jnp.sqrt(jnp.float32(Q)) * random_part


def block_scale(own_key, dims, cuts, low, high):
    def one(position, blocks):
        heights = jax.random.uniform(jax.random.fold_in(jax.random.fold_in(own_key, 6), position), (blocks,), jnp.float32, low / len(cuts), high / len(cuts))
        return jnp.repeat(jnp.exp(heights), dims[position] // blocks).reshape((-1,) + (1,) * (len(dims) - position - 1))

    level = one(*cuts[0])
    for cut in cuts[1:]:
        level = level * one(*cut)
    return level


def scatter_about(own_key, shape, scale, bound, cuts=(), held_as=jnp.bfloat16):
    gain = block_scale(own_key, shape, cuts, -0.22, 0.18) if cuts else 1.0
    array = jax.random.normal(own_key, shape, jnp.float32) * scale * gain
    return jnp.minimum(jnp.maximum(array, -bound), bound).astype(held_as)


def setup_inputs(seed: int = 0) -> dict:
    keys = jax.random.split(jax.random.key(seed), 7)
    initial = scatter_about(keys[0], (BRICKS, BRICK, ENS), 1.0, 6.0, ((0, 2),), jnp.float32)
    forcing = scatter_about(keys[1], (NT, BRICKS, BRICK, ENS), 0.5, 4.0, ((0, 16), (1, 2)))
    brick_blocks = draw_brick_blocks(jax.random.fold_in(keys[6], 71), 0)
    neighbours = draw_neighbours(jax.random.fold_in(keys[6], 71), 0)
    coarse_modes = scatter_about(keys[4], (Q, BRICK), BRICK ** -0.5, 0.75, (), jnp.float32)
    coarse_blocks = draw_coarse_blocks(jax.random.fold_in(keys[6], 71), 0)
    return {"initial": initial, "forcing": forcing, "brick_blocks": brick_blocks, "neighbours": neighbours, "coarse_modes": coarse_modes, "coarse_blocks": coarse_blocks}


highest = lax.Precision.HIGHEST


def rounded(values):
    return lax.optimization_barrier(values.astype(jnp.bfloat16)).astype(jnp.float32)


def propagate(values, diagonal, off_parts, neighbours):
    iterate = jnp.einsum("bij,sbje->sbie", diagonal, rounded(values))
    for sweep_index in range(SWEEPS - 1):
        source = rounded(iterate)
        coupled = jnp.zeros_like(values)
        for column in range(NB):
            coupled = coupled + jnp.einsum("bij,sbje->sbie", off_parts[column], source[:, neighbours[:, column]])
        iterate = jnp.einsum("bij,sbje->sbie", diagonal, rounded(values - coupled))
    return iterate


def reference(initial, forcing, brick_blocks, neighbours, coarse_modes, coarse_blocks):
    blocks = brick_blocks.astype(jnp.float32)
    diagonal = blocks[:, :, :BRICK]
    off_parts = [blocks[:, :, BRICK * (column + 1):BRICK * (column + 2)] for column in range(NB)]
    forcing_steps = forcing.reshape(N_TM, STEPS, BRICKS, BRICK, ENS)
    slice_ends = jnp.zeros((N_TM, BRICKS, BRICK, ENS), jnp.float32)
    slice_starts = jnp.concatenate([initial[None], slice_ends[:-1]], 0)

    def coarse_step(carried, new_term):
        follow = jnp.einsum("bpq,bqe->bpe", coarse_blocks, carried, precision=highest) + new_term
        return follow, follow

    defect = slice_ends
    for count_iter in range(ITERS):
        current = slice_starts
        for substep in range(STEPS - 1):
            current = propagate(current, diagonal, off_parts, neighbours) + forcing_steps[:, substep].astype(jnp.float32)
        defect = propagate(current, diagonal, off_parts, neighbours) + forcing_steps[:, STEPS - 1].astype(jnp.float32) - slice_ends
        restricted = jnp.einsum("qc,sbce->sbqe", coarse_modes, defect, precision=highest)
        start_error = jnp.zeros((BRICKS, Q, ENS), jnp.float32)
        final_error, errors = lax.scan(coarse_step, start_error, restricted)
        slice_ends = slice_ends + jnp.einsum("qc,sbqe->sbce", coarse_modes, errors, precision=highest)
        slice_starts = jnp.concatenate([initial[None], slice_ends[:-1]], 0)
    outputs = []
    current = slice_starts
    for substep in range(STEPS - 1):
        current = propagate(current, diagonal, off_parts, neighbours) + forcing_steps[:, substep].astype(jnp.float32)
        outputs.append(current)
    outputs.append(slice_ends)
    solution = jnp.stack(outputs, 1).reshape(NT, BRICKS, BRICK, ENS)
    return solution, defect
```

```python
import functools

import jax
import jax.numpy as jnp
from jax import lax
from jax.experimental import pallas as pl
from jax.experimental.pallas import tpu as pltpu
from jax.sharding import PartitionSpec as P

BRICK = 64
REACH = 4
Q = 8
SWEEPS = 3
STEPS = 4
ITERS = 2
GROUP = REACH

highest = lax.Precision.HIGHEST
f32 = jnp.float32
bf16 = jnp.bfloat16
VMEM = pl.BlockSpec(memory_space=pltpu.VMEM)
SMEM = pl.BlockSpec(memory_space=pltpu.SMEM)


def extended(block, sides, width):
    for axis, dim in sides:
        count = lax.axis_size(axis)
        forward = [(i, i + 1) for i in range(count - 1)]
        forward.append((count - 1, 0))
        backward = [(target, source) for source, target in forward]
        low = lax.ppermute(
            lax.slice_in_dim(block, block.shape[dim] - width, None, axis=dim), axis, forward
        )
        high = lax.ppermute(lax.slice_in_dim(block, 0, width, axis=dim), axis, backward)
        block = jnp.concatenate([low, block, high], axis=dim)
    return block


def carried_in(part, axis, combine, identity):
    place = lax.axis_index(axis)
    gathered = jax.tree.map(lambda a: lax.all_gather(a, axis), part)
    state = jax.tree.map(lambda a, e: jnp.zeros_like(a) + jnp.asarray(e, a.dtype), part, identity)

    def one(turn, state):
        return combine(
            state, jax.tree.map(lambda a: lax.dynamic_index_in_dim(a, turn, 0, False), gathered)
        )

    return lax.fori_loop(0, place, one, state)


def from_behind(block, axis, distance):
    devices = range(lax.axis_size(axis))
    route = [(i - distance, i) for i in devices if i - distance in devices]
    return lax.ppermute(block, axis, route)


def apply_inverse(diag_blocks, values):
    return jnp.einsum(
        "bij,bje->bie", diag_blocks, values.astype(jnp.bfloat16), preferred_element_type=jnp.float32
    )


def coupling(off_blocks, source, positions):
    picked = jnp.take(source, positions, axis=0)
    merged = picked.reshape(
        positions.shape[0], positions.shape[1] * source.shape[1], source.shape[2]
    )
    return jnp.einsum("bim,bme->bie", off_blocks, merged, preferred_element_type=jnp.float32)


def wrapped_offsets(indices, first_row, bricks_all):
    row_ids = jnp.arange(indices.shape[0], dtype=jnp.int32)
    position = jnp.mod(first_row + row_ids, bricks_all)
    return jnp.mod(indices - position[:, None] + REACH, bricks_all) - REACH


def banded_body(initial, forcing, brick_blocks, neighbours, coarse_modes, coarse_blocks):
    bricks_here = initial.shape[0]
    bricks_all = bricks_here * lax.axis_size("space")
    first_brick = lax.axis_index("space") * bricks_here
    slice_index = lax.axis_index("tm")
    own_shifts = wrapped_offsets(neighbours, first_brick, bricks_all)
    where_from = jnp.arange(bricks_here, dtype=jnp.int32)[:, None] + REACH + own_shifts
    diagonal = brick_blocks[:, :, :BRICK]
    off_blocks = brick_blocks[:, :, BRICK:]

    def propagate(values):
        iterate = apply_inverse(diagonal, values)
        for sweep_index in range(1, SWEEPS):
            rimmed = extended(iterate.astype(jnp.bfloat16), (("space", 0),), REACH)
            iterate = apply_inverse(diagonal, values - coupling(off_blocks, rimmed, where_from))
        return iterate

    is_first = slice_index == 0
    slice_starts = jnp.where(is_first, initial, jnp.zeros_like(initial))
    slice_ends = jnp.zeros_like(initial)
    identity = jnp.broadcast_to(jnp.eye(Q, dtype=jnp.float32), coarse_blocks.shape)
    nothing = jnp.zeros((bricks_here, Q, initial.shape[2]), jnp.float32)

    def compose(earlier, later):
        matrix = jnp.einsum("bpq,bqr->bpr", later[0], earlier[0], precision=highest)
        offset = jnp.einsum("bpq,bqe->bpe", later[0], earlier[1], precision=highest) + later[1]
        return (matrix, offset)

    defect = slice_ends
    for count_iter in range(ITERS):
        current = slice_starts
        for substep in range(STEPS - 1):
            current = propagate(current) + forcing[substep].astype(jnp.float32)
        defect = propagate(current) + forcing[STEPS - 1].astype(jnp.float32) - slice_ends
        restricted = jnp.einsum("qc,bce->bqe", coarse_modes, defect, precision=highest)
        prefix = carried_in((coarse_blocks, restricted), "tm", compose, (identity, nothing))
        before = prefix[1]
        corrected = (
            jnp.einsum("bpq,bqe->bpe", coarse_blocks, before, precision=highest) + restricted
        )
        slice_ends = slice_ends + jnp.einsum(
            "qc,bqe->bce", coarse_modes, corrected, precision=highest
        )
        shifted = from_behind(slice_ends.astype(jnp.bfloat16), "tm", 1).astype(slice_ends.dtype)
        slice_starts = jnp.where(is_first, initial, shifted)
    outputs = []
    current = slice_starts
    for substep in range(STEPS - 1):
        current = propagate(current) + forcing[substep].astype(jnp.float32)
        outputs.append(current)
    outputs.append(slice_ends)
    return (jnp.stack(outputs, 0), defect[None])


def dot(a, b):
    return jnp.dot(a, b, preferred_element_type=f32)


def dot_f32(a, b):
    return jnp.dot(a, b, preferred_element_type=f32, precision=highest)


def operator_kernel(parts, bits, info, nbr, *refs):
    blocks = refs[:parts]
    modes_t, modes, coarse, phi, images, powers, shifts, off, diag, lin = refs[parts:]
    here = blocks[0].shape[0]
    bricks = here * parts
    rows = bricks * BRICK
    groups = bricks // GROUP
    span = GROUP * BRICK
    wide = rows // 128
    lane = lax.broadcasted_iota(jnp.int32, (BRICK, 128), 1)
    left = lane < BRICK
    off[...] = jnp.zeros_like(off)
    diag[...] = jnp.zeros_like(diag)
    for b in range(bricks):
        source = blocks[b // here]
        r = b % here
        slots = source.shape[2] // BRICK
        for s in range(slots):
            tile = source[r, :, pl.ds((s // 2) * 128, min(128, source.shape[2] - (s // 2) * 128))]
            tile = tile.astype(f32)[:, (s % 2) * BRICK:(s % 2 + 1) * BRICK]
            both = jnp.concatenate([tile, tile], axis=1)
            if s == 0:
                keep = left if b % 2 == 0 else jnp.logical_not(left)
                at = (b % GROUP) // 2
                diag[pl.ds(b * BRICK, BRICK), pl.ds(at * 128, 128)] = jnp.where(
                    keep, both, 0.0
                ).astype(bf16)
            else:
                place = nbr[b, s - 1]
                half = lax.rem(place, 2)
                keep = (lane // BRICK) == half
                at = lax.div(place, 2)
                old = off[at, pl.ds(b * BRICK, BRICK), :]
                off[at, pl.ds(b * BRICK, BRICK), :] = old + jnp.where(keep, both, 0.0).astype(bf16)

    def near(r, k):
        return (r - k) % groups in (0, 1, groups - 1)

    for k in range(groups):
        d = diag[pl.ds(k * span, span), :]
        for r in range(groups):
            if near(r, k):
                o = jnp.concatenate(
                    [off[k * (span // 128) + i, pl.ds(r * span, span), :] for i in range(span // 128)],
                    axis=1,
                )
                lin[pl.ds(r * span, span), pl.ds(k * span, span)] = dot(o, d).astype(bf16)
    for n in range(groups):
        for r in range(groups):
            acc = None
            for k in range(groups):
                if near(r, k) and near(k, n):
                    part = dot(
                        lin[pl.ds(r * span, span), pl.ds(k * span, span)],
                        lin[pl.ds(k * span, span), pl.ds(n * span, span)],
                    )
                    acc = part if acc is None else acc + part
            d = diag[pl.ds(r * span, span), :]
            body = -acc if acc is not None else None
            if near(r, n):
                first = lin[pl.ds(r * span, span), pl.ds(n * span, span)].astype(f32)
                body = first if body is None else first + body
            out = jnp.zeros((span, span), f32) if body is None else -dot(d, body.astype(bf16))
            if r == n:
                out = out + d.astype(f32)
            phi[pl.ds(r * span, span), pl.ds(n * span, span)] = out.astype(bf16)
    own = here * BRICK
    image = modes_t[...]
    for i in range(STEPS):
        full = dot(phi[...], image)
        image = full.astype(bf16)
        images[i] = image[:own]
    size = bricks * Q
    a = coarse[...]
    m = modes[...]
    k = dot_f32(m, full)
    gram = lax.dot_general(m, m, (((1,), (1,)), ((), ())), preferred_element_type=f32, precision=highest)
    lower = k - dot_f32(gram, a)
    step = jnp.concatenate(
        [
            jnp.concatenate([a, jnp.zeros((size, size), f32)], axis=1),
            jnp.concatenate([lower, a], axis=1),
        ],
        axis=0,
    )
    row = lax.broadcasted_iota(jnp.int32, (2 * size, 2 * size), 0)
    col = lax.broadcasted_iota(jnp.int32, (2 * size, 2 * size), 1)
    moved = (row == col).astype(f32)
    for i in range(bits):
        powers[i] = step
        bit = info[i]
        shifts[i] = moved * (bit == 1).astype(f32)
        if i < bits - 1:
            moved = jnp.where(bit == 1, dot_f32(moved, step), moved)
            step = dot_f32(step, step)


def chain_kernel(parts, phi, first, force, modes, far_term, *refs):
    far_first = refs[:parts - 1]
    far_force = refs[parts - 1:2 * parts - 2]
    iterates, start = refs[2 * parts - 2:]
    own = first.shape[0]
    current = jnp.concatenate([first[...]] + [r[...] for r in far_first], axis=0)
    for i in range(STEPS - 1):
        full = dot(phi[...], current)
        mine = full[:own] + force[i].astype(f32)
        iterates[i] = mine
        current = jnp.concatenate(
            [mine.astype(bf16)]
            + [
                (full[own * (p + 1):own * (p + 2)] + far_force[p][i].astype(f32)).astype(bf16)
                for p in range(parts - 1)
            ],
            axis=0,
        )
    full = dot(phi[...], current)
    mine = full[:own] + force[STEPS - 1].astype(f32)
    iterates[STEPS - 1] = mine
    g = dot_f32(modes[...], jnp.concatenate([mine, full[own:]], axis=0)) + far_term[...]
    size = g.shape[0]
    m = modes[...]
    gram = lax.dot_general(m, m, (((1,), (1,)), ((), ())), preferred_element_type=f32, precision=highest)
    start[pl.ds(0, size), :] = g
    start[pl.ds(size, size), :] = g - dot_f32(gram, g)


def join_kernel(bit, power, shift, mine, other, before, total, prefix):
    upper = bit[0] == 1
    low = jnp.where(upper, other[...], mine[...])
    high = jnp.where(upper, mine[...], other[...])
    total[...] = dot_f32(power[...], low) + high
    prefix[...] = before[...] + dot_f32(shift[...], low)


def last_kernel(shift, other, before, step, start, images, modes_t, iterates, solution, defect):
    prefix = before[...] + dot_f32(shift[...], other[...])
    size = prefix.shape[0] // 2
    here = defect.shape[0]
    mine = dot_f32(step[...], prefix) + start[...]
    first = mine[:size]
    both = first + mine[size:]
    m = modes_t[...]
    shape = defect.shape
    came = (prefix[:size] + prefix[size:]).astype(bf16)
    for i in range(STEPS - 1):
        solution[i] = (iterates[i] + dot(images[i], came)).reshape(shape)
    solution[STEPS - 1] = dot_f32(m, both).reshape(shape)
    defect[...] = (
        iterates[STEPS - 1] + dot(images[STEPS - 1], prefix[:size].astype(bf16)) - dot_f32(m, first)
    ).reshape(shape)


def dense_body(initial, forcing, brick_blocks, neighbours, coarse_modes, coarse_blocks):
    here = initial.shape[0]
    ens = initial.shape[2]
    parts = lax.axis_size("space")
    bricks = here * parts
    own = here * BRICK
    rows = bricks * BRICK
    slices = lax.axis_size("tm")
    bits = slices.bit_length() - 1
    first_brick = lax.axis_index("space") * here
    place = lax.axis_index("tm")

    def others(value):
        return [
            lax.ppermute(value, "space", [((s + k) % parts, s) for s in range(parts)])
            for k in range(1, parts)
        ]

    far_blocks = others(brick_blocks)
    force = forcing.reshape(STEPS, own, ens)
    last_term = jnp.einsum(
        "qc,bce->bqe", coarse_modes, forcing[STEPS - 1].astype(f32), precision=highest
    ).reshape(here * Q, ens)
    small = jnp.concatenate(
        [
            last_term,
            jnp.pad(coarse_blocks.reshape(here * Q, Q), ((0, 0), (0, ens - Q))),
            jnp.pad(neighbours.astype(f32), ((0, 0), (0, ens - neighbours.shape[1]))),
        ],
        axis=0,
    )
    far_small = others(small)
    far_force = others(force[:STEPS - 1])
    start_half = initial.astype(bf16).reshape(own, ens)
    far_first = [
        lax.ppermute(
            start_half, ("tm", "space"), [((s + k) % parts, s) for s in range(parts)]
        )
        for k in range(1, parts)
    ]
    first = jnp.where(place == 0, start_half, jnp.zeros_like(start_half))

    slots = neighbours.shape[1]
    nbr = jnp.concatenate(
        [neighbours] + [f[2 * here * Q:, :slots].astype(jnp.int32) for f in far_small], axis=0
    )
    nbr = jnp.mod(nbr - first_brick, bricks)
    coarse_all = jnp.concatenate(
        [coarse_blocks.reshape(here * Q, Q)] + [f[here * Q:2 * here * Q, :Q] for f in far_small],
        axis=0,
    )
    far_term = jnp.concatenate(
        [jnp.zeros_like(last_term)] + [f[:here * Q] for f in far_small], axis=0
    )
    size = bricks * Q
    grid_row = lax.broadcasted_iota(jnp.int32, (size, size), 0) // Q
    grid_col = lax.broadcasted_iota(jnp.int32, (size, size), 1) // Q
    coarse = jnp.where(grid_row == grid_col, jnp.tile(coarse_all, (1, bricks)), 0.0)
    mode_row = lax.broadcasted_iota(jnp.int32, (size, rows), 0) // Q
    mode_col = lax.broadcasted_iota(jnp.int32, (size, rows), 1) // BRICK
    modes = jnp.where(mode_row == mode_col, jnp.tile(coarse_modes, (bricks, bricks)), 0.0)
    modes_t = modes.T
    info = jnp.stack([(place >> i) & 1 for i in range(bits)]).astype(jnp.int32)

    sds = jax.ShapeDtypeStruct
    phi, images, powers, shifts = pl.pallas_call(
        functools.partial(operator_kernel, parts, bits),
        out_shape=(
            sds((rows, rows), bf16),
            sds((STEPS, own, size), bf16),
            sds((bits, 2 * size, 2 * size), f32),
            sds((bits, 2 * size, 2 * size), f32),
        ),
        in_specs=[SMEM, SMEM] + [VMEM] * (parts + 3),
        out_specs=(VMEM,) * 4,
        scratch_shapes=[
            pltpu.VMEM((rows // 128, rows, 128), bf16),
            pltpu.VMEM((rows, GROUP * BRICK), bf16),
            pltpu.VMEM((rows, rows), bf16),
        ],
        name="operator",
    )(info, nbr, brick_blocks, *far_blocks, modes_t.astype(bf16), modes, coarse)

    iterates, start = pl.pallas_call(
        functools.partial(chain_kernel, parts),
        out_shape=(sds((STEPS, own, ens), f32), sds((2 * size, ens), f32)),
        in_specs=[VMEM] * (5 + 2 * (parts - 1)),
        out_specs=(VMEM,) * 2,
        name="chain",
    )(phi, first, force, modes, far_term, *far_first, *far_force)

    total = start
    prefix = jnp.zeros_like(start)
    for i in range(bits):
        other = lax.ppermute(total, "tm", [(j, j ^ (1 << i)) for j in range(slices)])
        if i < bits - 1:
            total, prefix = pl.pallas_call(
                join_kernel,
                out_shape=(sds((2 * size, ens), f32),) * 2,
                in_specs=[SMEM] + [VMEM] * 5,
                out_specs=(VMEM,) * 2,
                name="join",
            )(info[i:i + 1], powers[i], shifts[i], total, other, prefix)
    solution_out, defect = pl.pallas_call(
        last_kernel,
        out_shape=(sds((STEPS, here, BRICK, ens), f32), sds((here, BRICK, ens), f32)),
        in_specs=[VMEM] * 8,
        out_specs=(VMEM,) * 2,
        name="last",
    )(shifts[bits - 1], other, prefix, powers[0], start, images, modes_t[:own], iterates)
    return solution_out, defect[None]


def solution(mesh):
    placed = (
        P("space", None, None),
        P("tm", "space", None, None),
        P("space", None, None),
        P("space", None),
        P(),
        P("space", None, None),
    )

    def body(initial, *rest):
        bricks = initial.shape[0] * lax.axis_size("space")
        slices = lax.axis_size("tm")
        fits = 8 * (bricks * BRICK) ** 2 <= 16 * 2 ** 20
        even = bricks % GROUP == 0 and slices > 1 and slices & (slices - 1) == 0
        return (dense_body if fits and even else banded_body)(initial, *rest)

    return jax.shard_map(
        body,
        mesh=mesh,
        in_specs=placed,
        out_specs=(P("tm", "space", None, None), P("tm", "space", None, None)),
        check_vma=False,
    )
```

```python
import functools

import jax
import jax.numpy as jnp
from jax import lax
from jax.experimental import pallas as pl
from jax.experimental.pallas import tpu as pltpu
from jax.sharding import PartitionSpec as P

BRICK = 64
REACH = 4
Q = 8
SWEEPS = 3
STEPS = 4
ITERS = 2
GROUP = REACH

highest = lax.Precision.HIGHEST
f32 = jnp.float32
bf16 = jnp.bfloat16
VMEM = pl.BlockSpec(memory_space=pltpu.VMEM)
SMEM = pl.BlockSpec(memory_space=pltpu.SMEM)


def extended(block, sides, width):
    for axis, dim in sides:
        count = lax.axis_size(axis)
        forward = [(i, i + 1) for i in range(count - 1)]
        forward.append((count - 1, 0))
        backward = [(target, source) for source, target in forward]
        low = lax.ppermute(
            lax.slice_in_dim(block, block.shape[dim] - width, None, axis=dim), axis, forward
        )
        high = lax.ppermute(lax.slice_in_dim(block, 0, width, axis=dim), axis, backward)
        block = jnp.concatenate([low, block, high], axis=dim)
    return block


def carried_in(part, axis, combine, identity):
    place = lax.axis_index(axis)
    gathered = jax.tree.map(lambda a: lax.all_gather(a, axis), part)
    state = jax.tree.map(lambda a, e: jnp.zeros_like(a) + jnp.asarray(e, a.dtype), part, identity)

    def one(turn, state):
        return combine(
            state, jax.tree.map(lambda a: lax.dynamic_index_in_dim(a, turn, 0, False), gathered)
        )

    return lax.fori_loop(0, place, one, state)


def from_behind(block, axis, distance):
    devices = range(lax.axis_size(axis))
    route = [(i - distance, i) for i in devices if i - distance in devices]
    return lax.ppermute(block, axis, route)


def apply_inverse(diag_blocks, values):
    return jnp.einsum(
        "bij,bje->bie", diag_blocks, values.astype(jnp.bfloat16), preferred_element_type=jnp.float32
    )


def coupling(off_blocks, source, positions):
    picked = jnp.take(source, positions, axis=0)
    merged = picked.reshape(
        positions.shape[0], positions.shape[1] * source.shape[1], source.shape[2]
    )
    return jnp.einsum("bim,bme->bie", off_blocks, merged, preferred_element_type=jnp.float32)


def wrapped_offsets(indices, first_row, bricks_all):
    row_ids = jnp.arange(indices.shape[0], dtype=jnp.int32)
    position = jnp.mod(first_row + row_ids, bricks_all)
    return jnp.mod(indices - position[:, None] + REACH, bricks_all) - REACH


def banded_body(initial, forcing, brick_blocks, neighbours, coarse_modes, coarse_blocks):
    bricks_here = initial.shape[0]
    bricks_all = bricks_here * lax.axis_size("space")
    first_brick = lax.axis_index("space") * bricks_here
    slice_index = lax.axis_index("tm")
    own_shifts = wrapped_offsets(neighbours, first_brick, bricks_all)
    where_from = jnp.arange(bricks_here, dtype=jnp.int32)[:, None] + REACH + own_shifts
    diagonal = brick_blocks[:, :, :BRICK]
    off_blocks = brick_blocks[:, :, BRICK:]

    def propagate(values):
        iterate = apply_inverse(diagonal, values)
        for sweep_index in range(1, SWEEPS):
            rimmed = extended(iterate.astype(jnp.bfloat16), (("space", 0),), REACH)
            iterate = apply_inverse(diagonal, values - coupling(off_blocks, rimmed, where_from))
        return iterate

    is_first = slice_index == 0
    slice_starts = jnp.where(is_first, initial, jnp.zeros_like(initial))
    slice_ends = jnp.zeros_like(initial)
    identity = jnp.broadcast_to(jnp.eye(Q, dtype=jnp.float32), coarse_blocks.shape)
    nothing = jnp.zeros((bricks_here, Q, initial.shape[2]), jnp.float32)

    def compose(earlier, later):
        matrix = jnp.einsum("bpq,bqr->bpr", later[0], earlier[0], precision=highest)
        offset = jnp.einsum("bpq,bqe->bpe", later[0], earlier[1], precision=highest) + later[1]
        return (matrix, offset)

    defect = slice_ends
    for count_iter in range(ITERS):
        current = slice_starts
        for substep in range(STEPS - 1):
            current = propagate(current) + forcing[substep].astype(jnp.float32)
        defect = propagate(current) + forcing[STEPS - 1].astype(jnp.float32) - slice_ends
        restricted = jnp.einsum("qc,bce->bqe", coarse_modes, defect, precision=highest)
        prefix = carried_in((coarse_blocks, restricted), "tm", compose, (identity, nothing))
        before = prefix[1]
        corrected = (
            jnp.einsum("bpq,bqe->bpe", coarse_blocks, before, precision=highest) + restricted
        )
        slice_ends = slice_ends + jnp.einsum(
            "qc,bqe->bce", coarse_modes, corrected, precision=highest
        )
        shifted = from_behind(slice_ends.astype(jnp.bfloat16), "tm", 1).astype(slice_ends.dtype)
        slice_starts = jnp.where(is_first, initial, shifted)
    outputs = []
    current = slice_starts
    for substep in range(STEPS - 1):
        current = propagate(current) + forcing[substep].astype(jnp.float32)
        outputs.append(current)
    outputs.append(slice_ends)
    return (jnp.stack(outputs, 0), defect[None])


def dot(a, b):
    return jnp.dot(a, b, preferred_element_type=f32)


def dot_f32(a, b):
    return jnp.dot(a, b, preferred_element_type=f32, precision=highest)


def high_low(a):
    high = a.astype(bf16)
    return high, (a - high.astype(f32)).astype(bf16)


def dot_split(a, b):
    a_high, a_low = high_low(a)
    b_high, b_low = high_low(b)
    return dot(a_high, b_high) + (dot(a_high, b_low) + dot(a_low, b_high))


def call(kernel, name, out_shape, in_specs, *args, scratch=(), flops=0, vmem=16):
    return pl.pallas_call(
        kernel,
        out_shape=out_shape,
        in_specs=in_specs,
        out_specs=jax.tree.map(lambda _: VMEM, out_shape),
        scratch_shapes=scratch,
        compiler_params=pltpu.CompilerParams(vmem_limit_bytes=vmem * 2 ** 20),
        cost_estimate=pl.CostEstimate(flops=flops, bytes_accessed=2 ** 20, transcendentals=0),
        name=name,
    )(*args)


def modes_kernel(modes, tall, both):
    rows, size = tall.shape[0], tall.shape[1] // 2
    bricks = size // Q
    r = modes[...]
    lane = lax.broadcasted_iota(jnp.int32, (Q, size), 1)
    row = lax.broadcasted_iota(jnp.int32, (Q, size), 0)
    pick = (lane % Q == row).astype(f32)
    spread = lax.dot_general(
        r, pick, (((0,), (0,)), ((), ())), preferred_element_type=f32, precision=highest
    )
    owner = lax.broadcasted_iota(jnp.int32, (BRICK, size), 1) // Q
    for b in range(bricks):
        high, low = high_low(jnp.where(owner == b, spread, 0.0))
        tall[pl.ds(b * BRICK, BRICK), :size] = high
        tall[pl.ds(b * BRICK, BRICK), size:] = low
    gram = lax.dot_general(
        r, r, (((1,), (1,)), ((), ())), preferred_element_type=f32, precision=highest
    )
    rest = r - dot_f32(gram, r)
    for at, value in enumerate((r, rest)):
        pair = jnp.concatenate([value, value], axis=1)
        stack = jnp.concatenate([pair] * bricks, axis=0)
        mine = lax.broadcasted_iota(jnp.int32, stack.shape, 0) // Q
        half = lax.broadcasted_iota(jnp.int32, stack.shape, 1) // BRICK
        for t in range(rows // 128):
            both[pl.ds(at * size, size), pl.ds(t * 128, 128)] = jnp.where(
                mine == 2 * t + half, stack, 0.0
            ).astype(bf16)


def operator_kernel(parts, info, nbr, own, *refs):
    count = 2 * (parts - 1)
    pieces = refs[:count]
    first = refs[count]
    far_first = refs[count + 1:count + parts]
    tall, phi, state, off, diag, lin, masks = refs[count + parts:]
    here = own.shape[0]
    bricks = here * parts
    groups = bricks // GROUP
    span = GROUP * BRICK
    lane = lax.broadcasted_iota(jnp.int32, (BRICK, 128), 1)
    masks[0] = (lane < BRICK).astype(f32).astype(bf16)
    masks[1] = (lane >= BRICK).astype(f32).astype(bf16)
    off[...] = jnp.zeros_like(off)
    diag[...] = jnp.zeros_like(diag)

    def place_brick(source, r, b, in_group):
        start = pl.multiple_of(b * BRICK, BRICK)
        slots = source.shape[2] // BRICK
        for s in range(slots):
            width = min(128, source.shape[2] - (s // 2) * 128)
            tile = source[r, :, pl.ds((s // 2) * 128, width)]
            tile = tile[:, (s % 2) * BRICK:(s % 2 + 1) * BRICK]
            double = jnp.concatenate([tile, tile], axis=1)
            if s == 0:
                diag[pl.ds(start, BRICK), pl.ds((in_group // 2) * 128, 128)] = (
                    double * masks[in_group % 2]
                )
            else:
                place = nbr[b, s - 1]
                at = lax.div(place, 2)
                off[at, pl.ds(start, BRICK), :] += double * masks[lax.rem(place, 2)]

    for b in range(here):
        place_brick(own, b, b, b % GROUP)
    half = here // 2
    core = info[0]
    for p in range(parts - 1):
        for j in range(half):
            base = here * (p + 1) + j
            place_brick(pieces[2 * p], j, base + half * core, j % GROUP)
            place_brick(pieces[2 * p + 1], j, base + half * (1 - core), j % GROUP)

    def near(r, k):
        return (r - k) % groups in (0, 1, groups - 1)

    for k in range(groups):
        d = diag[pl.ds(k * span, span), :]
        for r in range(groups):
            if near(r, k):
                o = jnp.concatenate(
                    [off[k * (span // 128) + i, pl.ds(r * span, span), :] for i in range(span // 128)],
                    axis=1,
                )
                lin[pl.ds(r * span, span), pl.ds(k * span, span)] = dot(o, d).astype(bf16)
    for n in range(groups):
        for r in range(groups):
            acc = None
            for k in range(groups):
                if near(r, k) and near(k, n):
                    part = dot(
                        lin[pl.ds(r * span, span), pl.ds(k * span, span)],
                        lin[pl.ds(k * span, span), pl.ds(n * span, span)],
                    )
                    acc = part if acc is None else acc + part
            d = diag[pl.ds(r * span, span), :]
            body = -acc if acc is not None else None
            if near(r, n):
                plain = lin[pl.ds(r * span, span), pl.ds(n * span, span)].astype(f32)
                body = plain if body is None else plain + body
            out = jnp.zeros((span, span), f32) if body is None else -dot(d, body.astype(bf16))
            if r == n:
                out = out + d.astype(f32)
            phi[pl.ds(r * span, span), pl.ds(n * span, span)] = out.astype(bf16)
    begin = jnp.concatenate([first[...]] + [r[...] for r in far_first], axis=0)
    size = tall.shape[1] // 2
    state[...] = dot(phi[...], jnp.concatenate([begin, tall[:, :size]], axis=1))


def chain_kernel(parts, phi, state, force, both, far_term, *refs):
    far_force = refs[:parts - 1]
    iterates, images, start, coarse_phi = refs[parts - 1:]
    own, ens = force.shape[1], force.shape[2]
    full = state[...]
    for i in range(STEPS):
        mine = full[:own, :ens] + force[i].astype(f32)
        iterates[i] = mine
        moved = full[:, ens:].astype(bf16)
        images[i] = moved[:own]
        rows = [mine.astype(bf16)]
        for p in range(parts - 1):
            far = full[own * (p + 1):own * (p + 2), :ens]
            if i < STEPS - 1:
                far = far + far_force[p][i].astype(f32)
            rows.append(far.astype(bf16))
        current = jnp.concatenate([jnp.concatenate(rows, axis=0), moved], axis=1)
        if i < STEPS - 1:
            full = dot(phi[...], current)
    got = dot(both[...], current)
    size = got.shape[0] // 2
    start[...] = got[:, :ens] + far_term[...]
    coarse_phi[...] = got[:size, ens:]


def recurrence_kernel(bits, info, modes, own_coarse, *refs):
    far_coarse = refs[:-1 - bits]
    coarse_phi = refs[-1 - bits]
    outs = refs[-bits:]
    size = coarse_phi.shape[0]
    lane = lax.broadcasted_iota(jnp.int32, (Q, size), 1)
    row = lax.broadcasted_iota(jnp.int32, (Q, size), 0)
    pick = (lane % Q == row).astype(f32)
    tall = jnp.concatenate([own_coarse[...]] + [r[...] for r in far_coarse], axis=0)
    same = (
        lax.broadcasted_iota(jnp.int32, (size, size), 0) // Q
        == lax.broadcasted_iota(jnp.int32, (size, size), 1) // Q
    )
    a = jnp.where(same, dot_f32(tall, pick), 0.0)
    r = modes[...]
    gram = lax.dot_general(
        r, r, (((1,), (1,)), ((), ())), preferred_element_type=f32, precision=highest
    )
    gram = jnp.where(same, jnp.concatenate([dot_f32(gram, pick)] * (size // Q), axis=0), 0.0)
    lower = coarse_phi[...] - dot_f32(gram, a)
    step = jnp.concatenate(
        [
            jnp.concatenate([a, jnp.zeros((size, size), f32)], axis=1),
            jnp.concatenate([lower, a], axis=1),
        ],
        axis=0,
    )
    at = lax.broadcasted_iota(jnp.int32, step.shape, 0)
    to = lax.broadcasted_iota(jnp.int32, step.shape, 1)
    moved = (at == to).astype(f32)
    for i in range(bits):
        bit = info[1 + i] == 1
        wide = 2 * size
        high, low = high_low(step)
        outs[i][pl.ds(0, wide), :wide] = high
        outs[i][pl.ds(0, wide), wide:] = low
        high, low = high_low(jnp.where(bit, moved, 0.0))
        outs[i][pl.ds(wide, wide), :wide] = high
        outs[i][pl.ds(wide, wide), wide:] = low
        if i < bits - 1:
            moved = jnp.where(bit, dot_split(moved, step), moved)
            step = dot_split(step, step)


def join_kernel(opening, info, powers, mine, other, *refs):
    total, prefix = refs[-2:]
    wide = mine.shape[0]
    upper = info[0] == 1
    own, came = mine[...].astype(bf16).astype(f32), other[...].astype(f32)
    low = jnp.where(upper, came, own).astype(bf16)
    high = jnp.where(upper, own, came)
    moved = dot(powers[...], jnp.concatenate([low, low], axis=0))
    total[...] = (moved[:wide] + high).astype(bf16)
    if opening:
        prefix[...] = moved[wide:]
    else:
        prefix[...] = refs[0][...] + moved[wide:]


def last_kernel(powers, other, before, step, start, images, tall, iterates, solution, defect):
    wide = before.shape[0]
    size = wide // 2
    shape = defect.shape
    came = other[...]
    prefix = before[...] + dot(powers[pl.ds(wide, wide), :], jnp.concatenate([came, came], axis=0))
    low = prefix.astype(bf16)
    mine = dot(step[pl.ds(0, wide), :], jnp.concatenate([low, low], axis=0)) + start[...]
    first = mine[:size].astype(bf16)
    both = (mine[:size] + mine[size:]).astype(bf16)
    sum_low = (prefix[:size] + prefix[size:]).astype(bf16)
    for i in range(STEPS - 1):
        solution[i] = (iterates[i] + dot(images[i], sum_low)).reshape(shape)
    m = tall[...]
    solution[STEPS - 1] = dot(m, jnp.concatenate([both, both], axis=0)).reshape(shape)
    defect[...] = (
        iterates[STEPS - 1]
        + dot(images[STEPS - 1], low[:size])
        - dot(m, jnp.concatenate([first, first], axis=0))
    ).reshape(shape)


def dense_body(initial, forcing, brick_blocks, neighbours, coarse_modes, coarse_blocks):
    here, _, ens = initial.shape
    parts = lax.axis_size("space")
    bricks = here * parts
    own = here * BRICK
    rows = bricks * BRICK
    size = bricks * Q
    slices = lax.axis_size("tm")
    bits = slices.bit_length() - 1
    first_brick = lax.axis_index("space") * here
    place = lax.axis_index("tm")
    sds = jax.ShapeDtypeStruct

    def others(value):
        return [
            lax.ppermute(value, "space", [((s + k) % parts, s) for s in range(parts)])
            for k in range(1, parts)
        ]

    def paired(value, bit):
        return lax.ppermute(value, "tm", [(j, j ^ (1 << bit)) for j in range(slices)])

    half = here // 2
    core = place % 2
    some = lax.dynamic_slice_in_dim(brick_blocks, core * half, half, axis=0)
    fetched = others(some)
    some, forcing = lax.optimization_barrier((some, forcing))
    pieces = [piece for f in fetched for piece in (f, paired(f, 0))]
    slots = neighbours.shape[1]
    small = jnp.concatenate(
        [
            coarse_blocks.reshape(here * Q, Q),
            jnp.pad(neighbours.astype(f32), ((0, 0), (0, Q - slots))),
        ],
        axis=0,
    )
    far_small = others(small)
    force = forcing.reshape(STEPS, own, ens)
    far_force = others(force[:STEPS - 1])
    start_half = initial.astype(bf16).reshape(own, ens)
    far_first = [
        lax.ppermute(
            start_half, ("tm", "space"), [((s + k) % parts, s) for s in range(parts)]
        )
        for k in range(1, parts)
    ]
    first = jnp.where(place == 0, start_half, jnp.zeros_like(start_half))
    last_term = jnp.einsum(
        "qc,bce->bqe", coarse_modes, forcing[STEPS - 1].astype(f32), precision=highest
    )
    gram = jnp.dot(coarse_modes, coarse_modes.T, precision=highest)
    rest_term = last_term - jnp.einsum("qp,bpe->bqe", gram, last_term, precision=highest)
    terms = jnp.stack([last_term, rest_term]).reshape(2, here * Q, ens)
    far_terms = others(terms)
    far_term = jnp.concatenate(
        [jnp.zeros_like(terms)] + far_terms, axis=1
    ).reshape(2 * size, ens)

    nbr = jnp.concatenate(
        [neighbours] + [f[here * Q:, :slots].astype(jnp.int32) for f in far_small], axis=0
    )
    nbr = jnp.mod(nbr - first_brick, bricks)
    info = jnp.stack([core] + [(place >> i) & 1 for i in range(bits)]).astype(jnp.int32)

    tall, both = call(
        modes_kernel,
        "modes",
        (sds((rows, 2 * size), bf16), sds((2 * size, rows), bf16)),
        [VMEM],
        coarse_modes,
    )
    phi, state = call(
        functools.partial(operator_kernel, parts),
        "operator",
        (sds((rows, rows), bf16), sds((rows, ens + size), f32)),
        [SMEM, SMEM] + [VMEM] * (3 * parts),
        info, nbr, brick_blocks, *pieces, first, *far_first, tall,
        scratch=[
            pltpu.VMEM((rows // 128, rows, 128), bf16),
            pltpu.VMEM((rows, GROUP * BRICK), bf16),
            pltpu.VMEM((rows, rows), bf16),
            pltpu.VMEM((2, BRICK, 128), bf16),
        ],
        flops=2 * 4 * rows * rows * ens,
    )
    iterates, images, start, coarse_phi = call(
        functools.partial(chain_kernel, parts),
        "chain",
        (
            sds((STEPS, own, ens), f32),
            sds((STEPS, own, size), bf16),
            sds((2 * size, ens), f32),
            sds((size, size), f32),
        ),
        [VMEM] * (4 + parts),
        phi, state, force, both, far_term, *far_force,
        flops=2 * 3 * rows * rows * (ens + size),
    )
    powers = call(
        functools.partial(recurrence_kernel, bits),
        "recurrence",
        tuple(sds((4 * size, 4 * size), bf16) for _ in range(bits)),
        [SMEM] + [VMEM] * (2 + parts),
        info, coarse_modes, coarse_blocks.reshape(here * Q, Q),
        *[f[:here * Q] for f in far_small], coarse_phi,
        flops=2 * 9 * (2 * size) ** 3,
    )
    total = start.astype(bf16)
    prefix = None
    for i in range(bits):
        other = paired(total, i)
        if i < bits - 1:
            total, prefix = call(
                functools.partial(join_kernel, prefix is None),
                "join",
                (sds((2 * size, ens), bf16), sds((2 * size, ens), f32)),
                [SMEM] + [VMEM] * (3 if prefix is None else 4),
                info[i + 1:i + 2], powers[i], total, other, *(() if prefix is None else (prefix,)),
            )
    solution_out, defect = call(
        last_kernel,
        "last",
        (sds((STEPS, here, BRICK, ens), f32), sds((here, BRICK, ens), f32)),
        [VMEM] * 8,
        powers[bits - 1], other, prefix, powers[0], start, images, tall[:own], iterates,
    )
    return solution_out, defect[None]


def solution(mesh):
    placed = (
        P("space", None, None),
        P("tm", "space", None, None),
        P("space", None, None),
        P("space", None),
        P(),
        P("space", None, None),
    )

    def body(initial, *rest):
        here = initial.shape[0]
        bricks = here * lax.axis_size("space")
        slices = lax.axis_size("tm")
        fits = 8 * (bricks * BRICK) ** 2 <= 16 * 2 ** 20
        even = here % (2 * GROUP) == 0 and slices > 2 and slices & (slices - 1) == 0
        return (dense_body if fits and even else banded_body)(initial, *rest)

    return jax.shard_map(
        body,
        mesh=mesh,
        in_specs=placed,
        out_specs=(P("tm", "space", None, None), P("tm", "space", None, None)),
        check_vma=False,
    )
```

```python
import functools

import jax
import jax.numpy as jnp
from jax import lax
from jax.experimental import pallas as pl
from jax.experimental.pallas import tpu as pltpu
from jax.sharding import PartitionSpec as P


BRICK = 64
REACH = 4
Q = 8
SWEEPS = 3
STEPS = 4
ITERS = 2
GROUP = REACH

highest = lax.Precision.HIGHEST
f32 = jnp.float32
bf16 = jnp.bfloat16
VMEM = pl.BlockSpec(memory_space=pltpu.VMEM)
SMEM = pl.BlockSpec(memory_space=pltpu.SMEM)
HBM = pl.BlockSpec(memory_space=pltpu.HBM)


def extended(block, sides, width):
    for axis, dim in sides:
        count = lax.axis_size(axis)
        forward = [(i, i + 1) for i in range(count - 1)]
        forward.append((count - 1, 0))
        backward = [(target, source) for source, target in forward]
        low = lax.ppermute(
            lax.slice_in_dim(block, block.shape[dim] - width, None, axis=dim), axis, forward
        )
        high = lax.ppermute(lax.slice_in_dim(block, 0, width, axis=dim), axis, backward)
        block = jnp.concatenate([low, block, high], axis=dim)
    return block


def carried_in(part, axis, combine, identity):
    place = lax.axis_index(axis)
    gathered = jax.tree.map(lambda a: lax.all_gather(a, axis), part)
    state = jax.tree.map(lambda a, e: jnp.zeros_like(a) + jnp.asarray(e, a.dtype), part, identity)

    def one(turn, state):
        return combine(
            state, jax.tree.map(lambda a: lax.dynamic_index_in_dim(a, turn, 0, False), gathered)
        )

    return lax.fori_loop(0, place, one, state)


def from_behind(block, axis, distance):
    devices = range(lax.axis_size(axis))
    route = [(i - distance, i) for i in devices if i - distance in devices]
    return lax.ppermute(block, axis, route)


def apply_inverse(diag_blocks, values):
    return jnp.einsum(
        "bij,bje->bie", diag_blocks, values.astype(jnp.bfloat16), preferred_element_type=jnp.float32
    )


def coupling(off_blocks, source, positions):
    picked = jnp.take(source, positions, axis=0)
    merged = picked.reshape(
        positions.shape[0], positions.shape[1] * source.shape[1], source.shape[2]
    )
    return jnp.einsum("bim,bme->bie", off_blocks, merged, preferred_element_type=jnp.float32)


def wrapped_offsets(indices, first_row, bricks_all):
    row_ids = jnp.arange(indices.shape[0], dtype=jnp.int32)
    position = jnp.mod(first_row + row_ids, bricks_all)
    return jnp.mod(indices - position[:, None] + REACH, bricks_all) - REACH


def banded_body(initial, forcing, brick_blocks, neighbours, coarse_modes, coarse_blocks):
    bricks_here = initial.shape[0]
    bricks_all = bricks_here * lax.axis_size("space")
    first_brick = lax.axis_index("space") * bricks_here
    slice_index = lax.axis_index("tm")
    own_shifts = wrapped_offsets(neighbours, first_brick, bricks_all)
    where_from = jnp.arange(bricks_here, dtype=jnp.int32)[:, None] + REACH + own_shifts
    diagonal = brick_blocks[:, :, :BRICK]
    off_blocks = brick_blocks[:, :, BRICK:]

    def propagate(values):
        iterate = apply_inverse(diagonal, values)
        for _ in range(1, SWEEPS):
            rimmed = extended(iterate.astype(jnp.bfloat16), (("space", 0),), REACH)
            iterate = apply_inverse(diagonal, values - coupling(off_blocks, rimmed, where_from))
        return iterate

    is_first = slice_index == 0
    slice_starts = jnp.where(is_first, initial, jnp.zeros_like(initial))
    slice_ends = jnp.zeros_like(initial)
    identity = jnp.broadcast_to(jnp.eye(Q, dtype=jnp.float32), coarse_blocks.shape)
    nothing = jnp.zeros((bricks_here, Q, initial.shape[2]), jnp.float32)

    def compose(earlier, later):
        matrix = jnp.einsum("bpq,bqr->bpr", later[0], earlier[0], precision=highest)
        offset = jnp.einsum("bpq,bqe->bpe", later[0], earlier[1], precision=highest) + later[1]
        return (matrix, offset)

    defect = slice_ends
    for _ in range(ITERS):
        current = slice_starts
        for substep in range(STEPS - 1):
            current = propagate(current) + forcing[substep].astype(jnp.float32)
        defect = propagate(current) + forcing[STEPS - 1].astype(jnp.float32) - slice_ends
        restricted = jnp.einsum("qc,bce->bqe", coarse_modes, defect, precision=highest)
        prefix = carried_in((coarse_blocks, restricted), "tm", compose, (identity, nothing))
        before = prefix[1]
        corrected = (
            jnp.einsum("bpq,bqe->bpe", coarse_blocks, before, precision=highest) + restricted
        )
        slice_ends = slice_ends + jnp.einsum(
            "qc,bqe->bce", coarse_modes, corrected, precision=highest
        )
        shifted = from_behind(slice_ends.astype(jnp.bfloat16), "tm", 1).astype(slice_ends.dtype)
        slice_starts = jnp.where(is_first, initial, shifted)
    outputs = []
    current = slice_starts
    for substep in range(STEPS - 1):
        current = propagate(current) + forcing[substep].astype(jnp.float32)
        outputs.append(current)
    outputs.append(slice_ends)
    return (jnp.stack(outputs, 0), defect[None])


def dot(a, b):
    return jnp.dot(a, b, preferred_element_type=f32)


def dot_f32(a, b):
    return jnp.dot(a, b, preferred_element_type=f32, precision=highest)


def high_low(a):
    high = a.astype(bf16)
    return high, (a - high.astype(f32)).astype(bf16)


def dot_split(a, b):
    a_high, a_low = high_low(a)
    b_high, b_low = high_low(b)
    return dot(a_high, b_high) + (dot(a_high, b_low) + dot(a_low, b_high))


def call(kernel, out_shape, in_specs, *args, scratch=(), flops=0, vmem=16, out_space=VMEM):
    return pl.pallas_call(
        kernel,
        out_shape=out_shape,
        in_specs=in_specs,
        out_specs=jax.tree.map(lambda _: out_space, out_shape),
        scratch_shapes=scratch,
        compiler_params=pltpu.CompilerParams(vmem_limit_bytes=vmem * 2 ** 20),
        cost_estimate=pl.CostEstimate(flops=flops, bytes_accessed=2 ** 20, transcendentals=0),
    )(*args)


def fetch(sems, *pairs):
    copies = [pltpu.make_async_copy(a, b, sems.at[i]) for i, (a, b) in enumerate(pairs)]
    for copy in copies:
        copy.start()
    return copies


def half_kernel(blocks, out, sems):
    half = out.shape[0]
    core = lax.rem(lax.axis_index("tm"), 2)
    fetch(sems, (blocks.at[pl.ds(core * half, half)], out))[0].wait()


def pack_kernel(coarse, neighbours, initial, forcing, small, half, first, force, held, slots, sems):
    copies = fetch(
        sems, (initial, held), (neighbours, slots), (coarse, small.at[pl.ds(0, coarse.shape[0])]),
        (forcing.at[pl.ds(0, force.shape[0])], force),
    )
    for copy in copies[:3]:
        copy.wait()
    small[coarse.shape[0]:, :slots.shape[1]] = slots[...].astype(f32)
    rounded = held[...].astype(bf16).reshape(half.shape)
    half[...] = rounded
    mine = jnp.where(lax.axis_index("tm") == 0, 1.0, 0.0).astype(f32)
    first[...] = (rounded.astype(f32) * mine).astype(bf16)
    copies[3].wait()


def prepare_kernel(
    nbr_in, modes_in, forcing, blocks, tall, both, late, off, diag, last, own, modes, nbr, masks, sems
):
    copies = fetch(
        sems, (blocks, own), (forcing.at[pl.ds(STEPS - 2, 2)], last), (modes_in, modes), (nbr_in, nbr)
    )
    set_masks(masks)
    off[...] = jnp.zeros_like(off)
    diag[...] = jnp.zeros_like(diag)
    copies[2].wait()
    rows, size = tall.shape[0], tall.shape[1] // 2
    bricks = size // Q
    r = modes[...]
    lane = lax.broadcasted_iota(jnp.int32, (Q, size), 1)
    row = lax.broadcasted_iota(jnp.int32, (Q, size), 0)
    pick = (lane % Q == row).astype(f32)
    spread = lax.dot_general(
        r, pick, (((0,), (0,)), ((), ())), preferred_element_type=f32, precision=highest
    )
    owner = lax.broadcasted_iota(jnp.int32, (BRICK, size), 1) // Q
    for b in range(bricks):
        high, low = high_low(jnp.where(owner == b, spread, 0.0))
        tall[pl.ds(b * BRICK, BRICK), :size] = high
        tall[pl.ds(b * BRICK, BRICK), size:] = low
    gram = lax.dot_general(
        r, r, (((1,), (1,)), ((), ())), preferred_element_type=f32, precision=highest
    )
    rest = r - dot_f32(gram, r)
    for at, value in enumerate((r, rest)):
        pair = jnp.concatenate([value, value], axis=1)
        stack = jnp.concatenate([pair] * bricks, axis=0)
        mine = lax.broadcasted_iota(jnp.int32, stack.shape, 0) // Q
        half = lax.broadcasted_iota(jnp.int32, stack.shape, 1) // BRICK
        for t in range(rows // 128):
            both[pl.ds(at * size, size), pl.ds(t * 128, 128)] = jnp.where(
                mine == 2 * t + half, stack, 0.0
            ).astype(bf16)
    copies[0].wait()
    copies[3].wait()
    here = own.shape[0]
    first_brick = lax.axis_index("space") * here
    for b in range(here):
        place_brick(own, b, nbr, b, first_brick, bricks, b, b % GROUP, off, diag, masks)
    copies[1].wait()
    rows_here = here * BRICK
    count = here * Q
    late[:rows_here, :] = last[0].reshape(rows_here, last.shape[3])
    value = last[1].reshape(rows_here, last.shape[3])
    for at in range(2):
        late[pl.ds(rows_here + at * count, count), :] = dot(
            both[pl.ds(at * size, count), :rows_here], value
        ).astype(bf16)


def place_brick(source, r, nbr, b, first_brick, bricks, row, in_group, off, diag, masks):
    start = row * BRICK if isinstance(row, int) else pl.multiple_of(row * BRICK, BRICK)
    slots = source.shape[2] // BRICK
    for s in range(slots):
        width = min(128, source.shape[2] - (s // 2) * 128)
        tile = source[r, :, pl.ds((s // 2) * 128, width)]
        tile = tile[:, (s % 2) * BRICK:(s % 2 + 1) * BRICK]
        double = jnp.concatenate([tile, tile], axis=1)
        if s == 0:
            diag[pl.ds(start, BRICK), pl.ds((in_group // 2) * 128, 128)] = (
                double * masks[in_group % 2]
            )
        else:
            place = lax.rem(nbr[b, s - 1] - first_brick + bricks, bricks)
            at = lax.div(place, 2)
            off[at, pl.ds(start, BRICK), :] += double * masks[lax.rem(place, 2)]


def set_masks(masks):
    lane = lax.broadcasted_iota(jnp.int32, (BRICK, 128), 1)
    masks[0] = (lane < BRICK).astype(f32).astype(bf16)
    masks[1] = (lane >= BRICK).astype(f32).astype(bf16)


def operator_kernel(parts, nbr, own_off, own_diag, *refs):
    count = 2 * (parts - 1)
    pieces = refs[:count]
    first = refs[count]
    far_first = refs[count + 1:count + parts]
    tall, phi, state, far_off, far_diag, lin, left, masks = refs[count + parts:]
    own = own_diag.shape[0]
    here = own // BRICK
    bricks = here * parts
    groups = bricks // GROUP
    span = GROUP * BRICK
    set_masks(masks)
    far_off[...] = jnp.zeros_like(far_off)
    far_diag[...] = jnp.zeros_like(far_diag)
    half = here // 2
    core = lax.rem(lax.axis_index("tm"), 2)
    first_brick = lax.axis_index("space") * here
    for p in range(parts - 1):
        for j in range(half):
            for piece, side in ((0, core), (1, 1 - core)):
                row = here * p + j + half * side
                place_brick(
                    pieces[2 * p + piece], j, nbr, row, first_brick, bricks, row, j % GROUP,
                    far_off, far_diag, masks,
                )

    def near(r, k):
        return (r - k) % groups in (0, 1, groups - 1)

    def off_tile(r, k):
        ref, at = (own_off, r * span) if r * span < own else (far_off, r * span - own)
        return jnp.concatenate(
            [ref[k * (span // 128) + i, pl.ds(at, span), :] for i in range(span // 128)], axis=1
        )

    def diag_tile(r):
        ref, at = (own_diag, r * span) if r * span < own else (far_diag, r * span - own)
        return ref[pl.ds(at, span), :]

    def at(r, k):
        return pl.ds(r * span, span), pl.ds(k * span, span)

    for k in range(groups):
        for r in range(groups):
            if near(r, k):
                lin[at(r, k)] = dot(off_tile(r, k), diag_tile(k)).astype(bf16)
                left[at(r, k)] = dot(diag_tile(r), lin[at(r, k)]).astype(bf16)
    for n in range(groups):
        for r in range(groups):
            out = None
            for k in range(groups):
                if near(r, k) and near(k, n):
                    part = dot(left[at(r, k)], lin[at(k, n)])
                    out = part if out is None else out + part
            if out is None:
                out = jnp.zeros((span, span), f32)
            if near(r, n):
                out = out - left[at(r, n)].astype(f32)
            if r == n:
                out = out + diag_tile(r).astype(f32)
            phi[at(r, n)] = out.astype(bf16)
    begin = jnp.concatenate([first[...]] + [r[...] for r in far_first], axis=0)
    size = tall.shape[1] // 2
    state[...] = dot(phi[...], jnp.concatenate([begin, tall[:, :size]], axis=1))


def advance(parts, full, force, far_force, i, iterates, images):
    own, ens = force.shape[1], force.shape[2]
    mine = full[:own, :ens] + force[i].astype(f32)
    iterates[0] = mine
    moved = full[:, ens:].astype(bf16)
    images[0] = moved[:own]
    rows = [mine.astype(bf16)]
    for p in range(parts - 1):
        far = full[own * (p + 1):own * (p + 2), :ens]
        if far_force is not None:
            far = far + far_force[p].astype(f32)
        rows.append(far.astype(bf16))
    return jnp.concatenate([jnp.concatenate(rows, axis=0), moved], axis=1)


def early_kernel(parts, phi, state, force, *refs):
    far_force = refs[:parts - 1]
    iterates, images, out = refs[parts - 1:]
    own, ens = force.shape[1], force.shape[2]
    full = state[...]
    for i in range(iterates.shape[0]):
        far = [r[i].reshape(own, ens) for r in far_force]
        current = advance(
            parts, full, force, far, i, iterates.at[pl.ds(i, 1)], images.at[pl.ds(i, 1)]
        )
        full = dot(phi[...], current)
    out[...] = full


def late_kernel(parts, phi, state, force, both, *refs):
    far_late = refs[:parts - 1]
    iterates, images, start, sent, coarse_phi = refs[parts - 1:]
    own, ens = force.shape[1], force.shape[2]
    far = [r[:own, :] for r in far_late]
    current = advance(
        parts, state[...], force, far, STEPS - 2, iterates.at[pl.ds(0, 1)], images.at[pl.ds(0, 1)]
    )
    full = dot(phi[...], current)
    current = advance(
        parts, full, force, None, STEPS - 1, iterates.at[pl.ds(1, 1)], images.at[pl.ds(1, 1)]
    )
    got = dot(both[...], current)
    size = got.shape[0] // 2
    each = size // parts
    begin = got[:, :ens] + jnp.concatenate(
        [
            part
            for at in range(2)
            for part in [jnp.zeros((each, ens), f32)]
            + [r[pl.ds(own + at * each, each), :].astype(f32) for r in far_late]
        ],
        axis=0,
    )
    start[...] = begin
    sent[...] = begin.astype(bf16)
    coarse_phi[...] = got[:size, ens:]


def write_powers(out, step, moved):
    wide = step.shape[0]
    for at, value in enumerate((step, moved)):
        high, low = high_low(value)
        out[pl.ds(at * wide, wide), :wide] = high
        out[pl.ds(at * wide, wide), wide:] = low


def unit(wide):
    at = lax.broadcasted_iota(jnp.int32, (wide, wide), 0)
    to = lax.broadcasted_iota(jnp.int32, (wide, wide), 1)
    return (at == to).astype(f32)


def bit_of_place(i):
    return lax.rem(lax.shift_right_logical(lax.axis_index("tm"), i), 2) == 1


def recurrence_kernel(modes, own_coarse, *refs):
    far_coarse = refs[:-3]
    coarse_phi, step_out, out = refs[-3:]
    size = coarse_phi.shape[0]
    lane = lax.broadcasted_iota(jnp.int32, (Q, size), 1)
    row = lax.broadcasted_iota(jnp.int32, (Q, size), 0)
    pick = (lane % Q == row).astype(f32)
    tall = jnp.concatenate([own_coarse[...]] + [r[:own_coarse.shape[0]] for r in far_coarse], axis=0)
    same = (
        lax.broadcasted_iota(jnp.int32, (size, size), 0) // Q
        == lax.broadcasted_iota(jnp.int32, (size, size), 1) // Q
    )
    a = jnp.where(same, dot_f32(tall, pick), 0.0)
    r = modes[...]
    gram = lax.dot_general(
        r, r, (((1,), (1,)), ((), ())), preferred_element_type=f32, precision=highest
    )
    gram = jnp.where(same, jnp.concatenate([dot_f32(gram, pick)] * (size // Q), axis=0), 0.0)
    lower = coarse_phi[...] - dot_split(gram, a)
    step = jnp.concatenate(
        [
            jnp.concatenate([a, jnp.zeros((size, size), f32)], axis=1),
            jnp.concatenate([lower, a], axis=1),
        ],
        axis=0,
    )
    step_out[...] = step
    write_powers(out, step, jnp.where(bit_of_place(0), unit(2 * size), 0.0))


def powers_kernel(bits, step_in, *outs):
    step = step_in[...]
    moved = unit(step.shape[0])
    for i in range(1, bits):
        moved = jnp.where(bit_of_place(i - 1), dot_split(moved, step), moved)
        step = dot_split(step, step)
        write_powers(outs[i - 1], step, jnp.where(bit_of_place(i), moved, 0.0))


def join_kernel(turn, powers, mine, other, *refs):
    total, prefix = refs[-2:]
    wide = mine.shape[0]
    upper = bit_of_place(turn)
    own, came = mine[...].astype(bf16).astype(f32), other[...].astype(f32)
    low = jnp.where(upper, came, own).astype(bf16)
    high = jnp.where(upper, own, came)
    moved = dot(powers[...], jnp.concatenate([low, low], axis=0))
    total[...] = (moved[:wide] + high).astype(bf16)
    if turn == 0:
        prefix[...] = moved[wide:]
    else:
        prefix[...] = refs[0][...] + moved[wide:]


def last_kernel(
    powers, other, before, step, start, tall, early_images, late_images, early, late,
    solution, defect, held, sems
):
    wide = before.shape[0]
    size = wide // 2
    shape = defect.shape

    def send(i, value):
        held[i] = value.reshape(shape)
        to = solution.at[i] if i < STEPS else defect
        copy = pltpu.make_async_copy(held.at[i], to, sems.at[i])
        copy.start()
        return copy

    came = other[...]
    prefix = before[...] + dot(powers[pl.ds(wide, wide), :], jnp.concatenate([came, came], axis=0))
    low = prefix.astype(bf16)
    sum_low = (prefix[:size] + prefix[size:]).astype(bf16)
    images = [early_images[i] for i in range(STEPS - 2)] + [late_images[i] for i in range(2)]
    iterates = [early.at[i] for i in range(STEPS - 2)] + [late.at[i] for i in range(2)]
    copies = [send(i, iterates[i][...] + dot(images[i], sum_low)) for i in range(STEPS - 1)]
    mine = dot(step[pl.ds(0, wide), :], jnp.concatenate([low, low], axis=0)) + start[...]
    first = mine[:size].astype(bf16)
    both = (mine[:size] + mine[size:]).astype(bf16)
    own = early.shape[1]
    m = tall[:own, :]
    copies.append(send(STEPS - 1, dot(m, jnp.concatenate([both, both], axis=0))))
    copies.append(send(
        STEPS,
        iterates[STEPS - 1][...]
        + dot(images[STEPS - 1], low[:size])
        - dot(m, jnp.concatenate([first, first], axis=0)),
    ))
    for copy in copies:
        copy.wait()


def dense_body(initial, forcing, brick_blocks, neighbours, coarse_modes, coarse_blocks):
    here, _, ens = initial.shape
    parts = lax.axis_size("space")
    bricks = here * parts
    own = here * BRICK
    rows = bricks * BRICK
    size = bricks * Q
    slices = lax.axis_size("tm")
    bits = slices.bit_length() - 1
    sds = jax.ShapeDtypeStruct

    def in_hbm(value):
        return pltpu.with_memory_space_constraint(value, pltpu.HBM)

    def others(value):
        return [
            lax.ppermute(value, "space", [((s + k) % parts, s) for s in range(parts)])
            for k in range(1, parts)
        ]

    def paired(value, bit):
        return lax.ppermute(value, "tm", [(j, j ^ (1 << bit)) for j in range(slices)])

    half = here // 2
    coarse = coarse_blocks.reshape(here * Q, Q)
    force = forcing.reshape(STEPS, own, ens)
    slots = neighbours.shape[1]
    some = call(
        half_kernel, sds((half,) + brick_blocks.shape[1:], bf16), [HBM],
        in_hbm(brick_blocks),
        scratch=[pltpu.SemaphoreType.DMA((1,))],
    )
    fetched = others(some)
    small, start_half, first, send_force = call(
        pack_kernel,
        (
            sds((here * Q + here, Q), f32),
            sds((own, ens), bf16),
            sds((own, ens), bf16),
            sds((STEPS - 2,) + forcing.shape[1:], bf16),
        ),
        [HBM] * 4,
        in_hbm(coarse), in_hbm(neighbours), in_hbm(initial), in_hbm(forcing),
        scratch=[
            pltpu.VMEM(initial.shape, f32),
            pltpu.VMEM(neighbours.shape, jnp.int32),
            pltpu.SemaphoreType.DMA((4,)),
        ],
    )
    far_small = others(small)
    far_first = [
        lax.ppermute(
            start_half, ("tm", "space"), [((s + k) % parts, s) for s in range(parts)]
        )
        for k in range(1, parts)
    ]
    far_force = others(send_force)
    tall, both, late, own_off, own_diag = call(
        prepare_kernel,
        (
            sds((rows, 2 * size), bf16),
            sds((2 * size, rows), bf16),
            sds((own + 2 * here * Q, ens), bf16),
            sds((rows // 128, own, 128), bf16),
            sds((own, GROUP * BRICK), bf16),
        ),
        [HBM] * 4,
        in_hbm(neighbours), in_hbm(coarse_modes), in_hbm(forcing), in_hbm(brick_blocks),
        scratch=[
            pltpu.VMEM((2,) + forcing.shape[1:], bf16),
            pltpu.VMEM(brick_blocks.shape, bf16),
            pltpu.VMEM(coarse_modes.shape, f32),
            pltpu.SMEM(neighbours.shape, jnp.int32),
            pltpu.VMEM((2, BRICK, 128), bf16),
            pltpu.SemaphoreType.DMA((4,)),
        ],
    )
    pieces = [piece for f in fetched for piece in (f, paired(f, 0))]
    far_late = others(late)
    far_nbr = [f[here * Q:, :slots].astype(jnp.int32) for f in far_small]
    far_nbr = far_nbr[0] if parts == 2 else jnp.concatenate(far_nbr, axis=0)
    phi, state = call(
        functools.partial(operator_kernel, parts),
        (sds((rows, rows), bf16), sds((rows, ens + size), f32)),
        [SMEM] + [VMEM] * (3 * parts + 1),
        far_nbr, own_off, own_diag, *pieces, first, *far_first, tall,
        scratch=[
            pltpu.VMEM((rows // 128, rows - own, 128), bf16),
            pltpu.VMEM((rows - own, GROUP * BRICK), bf16),
            pltpu.VMEM((rows, rows), bf16),
            pltpu.VMEM((rows, rows), bf16),
            pltpu.VMEM((2, BRICK, 128), bf16),
        ],
        flops=2 * 4 * rows * rows * ens,
        vmem=20,
    )
    early_iterates, early_images, state = call(
        functools.partial(early_kernel, parts),
        (
            sds((STEPS - 2, own, ens), f32),
            sds((STEPS - 2, own, size), bf16),
            sds((rows, ens + size), f32),
        ),
        [VMEM] * (2 + parts),
        phi, state, force, *far_force,
        flops=2 * 2 * rows * rows * (ens + size),
    )
    late_iterates, late_images, start, sent, coarse_phi = call(
        functools.partial(late_kernel, parts),
        (
            sds((2, own, ens), f32),
            sds((2, own, size), bf16),
            sds((2 * size, ens), f32),
            sds((2 * size, ens), bf16),
            sds((size, size), f32),
        ),
        [VMEM] * (3 + parts),
        phi, state, force, both, *far_late,
        flops=2 * rows * rows * (ens + size),
    )
    table = sds((4 * size, 4 * size), bf16)
    step, opening = call(
        recurrence_kernel,
        (sds((2 * size, 2 * size), f32), table),
        [VMEM] * (2 + parts),
        coarse_modes, coarse, *far_small, coarse_phi,
        flops=2 * 3 * (2 * size) ** 3,
    )
    powers = [opening] + list(call(
        functools.partial(powers_kernel, bits),
        (table,) * (bits - 1),
        [VMEM],
        step,
        flops=2 * 18 * (2 * size) ** 3,
    ))
    total = sent
    prefix = None
    for i in range(bits):
        other = paired(total, i)
        if i < bits - 1:
            total, prefix = call(
                functools.partial(join_kernel, i),
                (sds((2 * size, ens), bf16), sds((2 * size, ens), f32)),
                [VMEM] * (3 if prefix is None else 4),
                powers[i], total, other, *(() if prefix is None else (prefix,)),
            )
    solution_out, defect = call(
        last_kernel,
        (sds((STEPS, here, BRICK, ens), f32), sds((here, BRICK, ens), f32)),
        [VMEM] * 10,
        powers[bits - 1], other, prefix, powers[0], start, tall, early_images, late_images,
        early_iterates, late_iterates,
        scratch=[
            pltpu.VMEM((STEPS + 1, here, BRICK, ens), f32),
            pltpu.SemaphoreType.DMA((STEPS + 1,)),
        ],
        out_space=pl.BlockSpec(memory_space=pl.ANY),
    )
    return solution_out, defect[None]


def solution(mesh):
    placed = (
        P("space", None, None),
        P("tm", "space", None, None),
        P("space", None, None),
        P("space", None),
        P(),
        P("space", None, None),
    )

    def body(initial, *rest):
        here = initial.shape[0]
        bricks = here * lax.axis_size("space")
        slices = lax.axis_size("tm")
        fits = 8 * (bricks * BRICK) ** 2 <= 16 * 2 ** 20
        even = here % (2 * GROUP) == 0 and slices > 2 and slices & (slices - 1) == 0
        return (dense_body if fits and even else banded_body)(initial, *rest)

    return jax.shard_map(
        body,
        mesh=mesh,
        in_specs=placed,
        out_specs=(P("tm", "space", None, None), P("tm", "space", None, None)),
        check_vma=False,
    )
```

```python
import functools

import jax
import jax.numpy as jnp
from jax import lax
from jax.experimental import pallas as pl
from jax.experimental.pallas import tpu as pltpu
from jax.sharding import PartitionSpec as P


BRICK = 64
REACH = 4
Q = 8
SWEEPS = 3
STEPS = 4
ITERS = 2
GROUP = REACH

highest = lax.Precision.HIGHEST
f32 = jnp.float32
bf16 = jnp.bfloat16
VMEM = pl.BlockSpec(memory_space=pltpu.VMEM)
SMEM = pl.BlockSpec(memory_space=pltpu.SMEM)
HBM = pl.BlockSpec(memory_space=pltpu.HBM)


def extended(block, sides, width):
    for axis, dim in sides:
        count = lax.axis_size(axis)
        forward = [(i, i + 1) for i in range(count - 1)]
        forward.append((count - 1, 0))
        backward = [(target, source) for source, target in forward]
        low = lax.ppermute(
            lax.slice_in_dim(block, block.shape[dim] - width, None, axis=dim), axis, forward
        )
        high = lax.ppermute(lax.slice_in_dim(block, 0, width, axis=dim), axis, backward)
        block = jnp.concatenate([low, block, high], axis=dim)
    return block


def carried_in(part, axis, combine, identity):
    place = lax.axis_index(axis)
    gathered = jax.tree.map(lambda a: lax.all_gather(a, axis), part)
    state = jax.tree.map(lambda a, e: jnp.zeros_like(a) + jnp.asarray(e, a.dtype), part, identity)

    def one(turn, state):
        return combine(
            state, jax.tree.map(lambda a: lax.dynamic_index_in_dim(a, turn, 0, False), gathered)
        )

    return lax.fori_loop(0, place, one, state)


def from_behind(block, axis, distance):
    devices = range(lax.axis_size(axis))
    route = [(i - distance, i) for i in devices if i - distance in devices]
    return lax.ppermute(block, axis, route)


def apply_inverse(diag_blocks, values):
    return jnp.einsum(
        "bij,bje->bie", diag_blocks, values.astype(jnp.bfloat16), preferred_element_type=jnp.float32
    )


def coupling(off_blocks, source, positions):
    picked = jnp.take(source, positions, axis=0)
    merged = picked.reshape(
        positions.shape[0], positions.shape[1] * source.shape[1], source.shape[2]
    )
    return jnp.einsum("bim,bme->bie", off_blocks, merged, preferred_element_type=jnp.float32)


def wrapped_offsets(indices, first_row, bricks_all):
    row_ids = jnp.arange(indices.shape[0], dtype=jnp.int32)
    position = jnp.mod(first_row + row_ids, bricks_all)
    return jnp.mod(indices - position[:, None] + REACH, bricks_all) - REACH


def banded_body(initial, forcing, brick_blocks, neighbours, coarse_modes, coarse_blocks):
    bricks_here = initial.shape[0]
    bricks_all = bricks_here * lax.axis_size("space")
    first_brick = lax.axis_index("space") * bricks_here
    slice_index = lax.axis_index("tm")
    own_shifts = wrapped_offsets(neighbours, first_brick, bricks_all)
    where_from = jnp.arange(bricks_here, dtype=jnp.int32)[:, None] + REACH + own_shifts
    diagonal = brick_blocks[:, :, :BRICK]
    off_blocks = brick_blocks[:, :, BRICK:]

    def propagate(values):
        iterate = apply_inverse(diagonal, values)
        for _ in range(1, SWEEPS):
            rimmed = extended(iterate.astype(jnp.bfloat16), (("space", 0),), REACH)
            iterate = apply_inverse(diagonal, values - coupling(off_blocks, rimmed, where_from))
        return iterate

    is_first = slice_index == 0
    slice_starts = jnp.where(is_first, initial, jnp.zeros_like(initial))
    slice_ends = jnp.zeros_like(initial)
    identity = jnp.broadcast_to(jnp.eye(Q, dtype=jnp.float32), coarse_blocks.shape)
    nothing = jnp.zeros((bricks_here, Q, initial.shape[2]), jnp.float32)

    def compose(earlier, later):
        matrix = jnp.einsum("bpq,bqr->bpr", later[0], earlier[0], precision=highest)
        offset = jnp.einsum("bpq,bqe->bpe", later[0], earlier[1], precision=highest) + later[1]
        return (matrix, offset)

    defect = slice_ends
    for _ in range(ITERS):
        current = slice_starts
        for substep in range(STEPS - 1):
            current = propagate(current) + forcing[substep].astype(jnp.float32)
        defect = propagate(current) + forcing[STEPS - 1].astype(jnp.float32) - slice_ends
        restricted = jnp.einsum("qc,bce->bqe", coarse_modes, defect, precision=highest)
        prefix = carried_in((coarse_blocks, restricted), "tm", compose, (identity, nothing))
        before = prefix[1]
        corrected = (
            jnp.einsum("bpq,bqe->bpe", coarse_blocks, before, precision=highest) + restricted
        )
        slice_ends = slice_ends + jnp.einsum(
            "qc,bqe->bce", coarse_modes, corrected, precision=highest
        )
        shifted = from_behind(slice_ends.astype(jnp.bfloat16), "tm", 1).astype(slice_ends.dtype)
        slice_starts = jnp.where(is_first, initial, shifted)
    outputs = []
    current = slice_starts
    for substep in range(STEPS - 1):
        current = propagate(current) + forcing[substep].astype(jnp.float32)
        outputs.append(current)
    outputs.append(slice_ends)
    return (jnp.stack(outputs, 0), defect[None])


def dot(a, b):
    return jnp.dot(a, b, preferred_element_type=f32)


def dot_f32(a, b):
    return jnp.dot(a, b, preferred_element_type=f32, precision=highest)


def high_low(a):
    high = a.astype(bf16)
    return high, (a - high.astype(f32)).astype(bf16)


def dot_split(a, b):
    a_high, a_low = high_low(a)
    b_high, b_low = high_low(b)
    return dot(a_high, b_high) + (dot(a_high, b_low) + dot(a_low, b_high))


def call(kernel, out_shape, in_specs, *args, scratch=(), flops=0, vmem=16, out_space=VMEM):
    return pl.pallas_call(
        kernel,
        out_shape=out_shape,
        in_specs=in_specs,
        out_specs=jax.tree.map(lambda _: out_space, out_shape),
        scratch_shapes=scratch,
        compiler_params=pltpu.CompilerParams(vmem_limit_bytes=vmem * 2 ** 20),
        cost_estimate=pl.CostEstimate(flops=flops, bytes_accessed=2 ** 20, transcendentals=0),
    )(*args)


def unit(wide):
    at = lax.broadcasted_iota(jnp.int32, (wide, wide), 0)
    to = lax.broadcasted_iota(jnp.int32, (wide, wide), 1)
    return (at == to).astype(f32)


def fetch(sems, *pairs):
    copies = [pltpu.make_async_copy(a, b, sems.at[i]) for i, (a, b) in enumerate(pairs)]
    for copy in copies:
        copy.start()
    return copies


def half_kernel(blocks, nbr, out, held, slots, sems):
    half = held.shape[0]
    core = lax.rem(lax.axis_index("tm"), 2)
    whole = held.shape[2] // 128
    copies = fetch(
        sems, (nbr, slots), (blocks.at[pl.ds(core * half, half)], held),
    )
    here = slots.shape[0]
    top = half * (slots.shape[1] + 1) // 2 * BRICK
    copies[0].wait()
    out[top:, :] = jnp.zeros((out.shape[0] - top, 128), bf16)
    out[top:top + here, :slots.shape[1]] = slots[...].astype(f32).astype(bf16)
    copies[1].wait()
    for r in range(half):
        for t in range(whole):
            out[pl.ds((r * whole + t) * BRICK, BRICK), :] = held[r, :, pl.ds(t * 128, 128)]
    if held.shape[2] > whole * 128:
        for r in range(0, half, 2):
            out[pl.ds((half * whole + r // 2) * BRICK, BRICK), :] = jnp.concatenate(
                [held[r + i, :, pl.ds(whole * 128, BRICK)] for i in range(2)], axis=1
            )


def pack_kernel(initial, forcing, half, first, force, held, sems):
    copies = fetch(sems, (initial, held), (forcing.at[pl.ds(0, STEPS - 2)], force))
    copies[0].wait()
    rounded = held[...].astype(bf16).reshape(half.shape)
    half[...] = rounded
    mine = jnp.where(lax.axis_index("tm") == 0, 1.0, 0.0).astype(f32)
    first[...] = (rounded.astype(f32) * mine).astype(bf16)
    for copy in copies[1:]:
        copy.wait()


def packed_tile(piece, half, slots, r, s):
    whole = slots // 2
    at, side = (r * whole + s // 2, s % 2) if s // 2 < whole else (half * whole + r // 2, r % 2)
    return piece[pl.ds(at * BRICK, BRICK), :][:, side * BRICK:(side + 1) * BRICK]


def plain_tile(blocks, r, s):
    width = min(128, blocks.shape[2] - (s // 2) * 128)
    pair = blocks[r, :, pl.ds((s // 2) * 128, width)]
    return pair[:, (s % 2) * BRICK:(s % 2 + 1) * BRICK]


def prepare_kernel(
    nbr_in, modes_in, coarse_in, forcing, blocks, tall, both, extra, late, off, diag, gram_out,
    force, coarse,
    last, own, modes, nbr, masks, sems,
):
    copies = fetch(
        sems, (blocks, own), (forcing.at[pl.ds(STEPS - 2, 2)], last), (modes_in, modes), (nbr_in, nbr),
        (coarse_in, coarse),
    )
    set_masks(masks)
    off[...] = jnp.zeros_like(off)
    diag[...] = jnp.zeros_like(diag)
    copies[2].wait()
    rows, size = tall.shape[0], tall.shape[1] // 2
    bricks = size // Q
    r = modes[...]
    lane = lax.broadcasted_iota(jnp.int32, (Q, size), 1)
    row = lax.broadcasted_iota(jnp.int32, (Q, size), 0)
    pick = (lane % Q == row).astype(f32)
    spread = lax.dot_general(
        r, pick, (((0,), (0,)), ((), ())), preferred_element_type=f32, precision=highest
    )
    owner = lax.broadcasted_iota(jnp.int32, (BRICK, size), 1) // Q
    for b in range(bricks):
        high, low = high_low(jnp.where(owner == b, spread, 0.0))
        tall[pl.ds(b * BRICK, BRICK), :size] = high
        tall[pl.ds(b * BRICK, BRICK), size:] = low
    gram = lax.dot_general(
        r, r, (((1,), (1,)), ((), ())), preferred_element_type=f32, precision=highest
    )
    same = (
        lax.broadcasted_iota(jnp.int32, (size, size), 0) // Q
        == lax.broadcasted_iota(jnp.int32, (size, size), 1) // Q
    )
    gram_out[...] = jnp.where(same, jnp.concatenate([dot_f32(gram, pick)] * bricks, axis=0), 0.0)
    pair = jnp.concatenate([r, r], axis=1)
    stack = jnp.concatenate([pair] * bricks, axis=0)
    mine = lax.broadcasted_iota(jnp.int32, stack.shape, 0) // Q
    half = lax.broadcasted_iota(jnp.int32, stack.shape, 1) // BRICK
    for t in range(rows // 128):
        both[:, pl.ds(t * 128, 128)] = jnp.where(mine == 2 * t + half, stack, 0.0).astype(bf16)
    copies[0].wait()
    copies[3].wait()
    here = own.shape[0]
    first_brick = lax.axis_index("space") * here
    for b in range(here):
        tiles = [plain_tile(own, b, s) for s in range(nbr.shape[1] + 1)]
        place_brick(tiles, nbr, b, first_brick, bricks, b, b % GROUP, off, diag, masks)
    copies[1].wait()
    rows_here = here * BRICK
    count = here * Q
    late[...] = last[0].reshape(rows_here, last.shape[3])
    value = last[1].reshape(rows_here, last.shape[3])
    force[...] = value
    extra[:count, :] = dot(both[pl.ds(0, count), :rows_here], value).astype(bf16)
    copies[4].wait()
    turned = lax.dot_general(
        coarse[...], unit(count), (((0,), (0,)), ((), ())),
        preferred_element_type=f32, precision=highest,
    )
    pair = jnp.concatenate([v.astype(f32) for v in high_low(turned)], axis=1)
    extra[count:, :] = pair.astype(bf16)


def place_brick(tiles, nbr, b, first_brick, bricks, row, in_group, off, diag, masks):
    start = row * BRICK if isinstance(row, int) else pl.multiple_of(row * BRICK, BRICK)
    for s, tile in enumerate(tiles):
        double = jnp.concatenate([tile, tile], axis=1)
        if s == 0:
            diag[pl.ds(start, BRICK), pl.ds((in_group // 2) * 128, 128)] = (
                double * masks[in_group % 2]
            )
        else:
            place = lax.rem(nbr[b, s - 1] - first_brick + bricks, bricks)
            at = lax.div(place, 2)
            off[at, pl.ds(start, BRICK), :] += double * masks[lax.rem(place, 2)]


def set_masks(masks):
    lane = lax.broadcasted_iota(jnp.int32, (BRICK, 128), 1)
    masks[0] = (lane < BRICK).astype(f32).astype(bf16)
    masks[1] = (lane >= BRICK).astype(f32).astype(bf16)


def near(r, k, groups):
    return (r - k) % groups in (0, 1, groups - 1)


def tile_at(r, k):
    span = GROUP * BRICK
    return pl.ds(r * span, span), pl.ds(k * span, span)


def joined_tile(off, row, k):
    span = GROUP * BRICK
    return jnp.concatenate(
        [off[k * (span // 128) + i, pl.ds(row, span), :] for i in range(span // 128)], axis=1
    )


def first_kernel(parts, nbr, own_off, own_diag, *refs):
    pieces = refs[:parts - 1]
    offs = refs[parts - 1:2 * parts - 2]
    diags = refs[2 * parts - 2:3 * parts - 3]
    lin, left, product, masks = refs[3 * parts - 3:]
    own = own_diag.shape[0]
    here = own // BRICK
    bricks = here * parts
    span = GROUP * BRICK
    groups = bricks // GROUP
    owned = own // span
    set_masks(masks)
    half = here // 2
    core = lax.rem(lax.axis_index("tm"), 2)
    first_brick = lax.axis_index("space") * here
    slots = nbr.shape[1] + 1
    for p in range(parts - 1):
        offs[p][...] = jnp.zeros_like(offs[p])
        diags[p][...] = jnp.zeros_like(diags[p])
        for j in range(half):
            tiles = [packed_tile(pieces[p], half, slots, j, s) for s in range(slots)]
            place_brick(
                tiles, nbr, here * p + half * core + j, first_brick, bricks, j, j % GROUP,
                offs[p], diags[p], masks,
            )
    for k in range(owned):
        for r in range(owned):
            if near(r, k, groups):
                m = dot(joined_tile(own_off, r * span, k), own_diag[pl.ds(k * span, span), :])
                lin[tile_at(r, k)] = m.astype(bf16)
                left[tile_at(r, k)] = dot(
                    own_diag[pl.ds(r * span, span), :], lin[tile_at(r, k)]
                ).astype(bf16)
    for n in range(owned):
        for r in range(owned):
            out = jnp.zeros((span, span), f32)
            for k in range(owned):
                if near(r, k, groups) and near(k, n, groups):
                    out = out + dot(left[tile_at(r, k)], lin[tile_at(k, n)])
            product[tile_at(r, n)] = out


def operator_kernel(parts, nbr, own_off, own_diag, own_lin, own_left, own_product, *refs):
    pieces = refs[:parts - 1]
    offs = refs[parts - 1:2 * parts - 2]
    diags = refs[2 * parts - 2:3 * parts - 3]
    phi, far_off, far_diag, lin, left, masks = refs[3 * parts - 3:]
    own = own_diag.shape[0]
    here = own // BRICK
    bricks = here * parts
    groups = bricks // GROUP
    span = GROUP * BRICK
    owned = own // span
    set_masks(masks)
    half = here // 2
    core = lax.rem(lax.axis_index("tm"), 2)
    first_brick = lax.axis_index("space") * here
    slots = nbr.shape[1] + 1
    tall = half * BRICK
    for p in range(parts - 1):
        mine = pl.ds(pl.multiple_of((here * p + half * core) * BRICK, tall), tall)
        other = pl.ds(pl.multiple_of((here * p + half * (1 - core)) * BRICK, tall), tall)
        far_off[:, mine, :] = offs[p][...]
        far_diag[mine, :] = diags[p][...]
        far_off[:, other, :] = jnp.zeros((far_off.shape[0], tall, 128), bf16)
        far_diag[other, :] = jnp.zeros((tall, span), bf16)
        for j in range(half):
            row = here * p + j + half * (1 - core)
            tiles = [packed_tile(pieces[p], half, slots, j, s) for s in range(slots)]
            place_brick(
                tiles, nbr, row, first_brick, bricks, row, j % GROUP, far_off, far_diag, masks
            )

    def off_tile(r, k):
        if r < owned:
            return joined_tile(own_off, r * span, k)
        return joined_tile(far_off, r * span - own, k)

    def diag_tile(r):
        ref, at = (own_diag, r * span) if r < owned else (far_diag, r * span - own)
        return ref[pl.ds(at, span), :]

    def lin_tile(r, k):
        return (own_lin if r < owned and k < owned else lin)[tile_at(r, k)]

    def left_tile(r, k):
        return (own_left if r < owned and k < owned else left)[tile_at(r, k)]

    for k in range(groups):
        for r in range(groups):
            if near(r, k, groups) and not (r < owned and k < owned):
                lin[tile_at(r, k)] = dot(off_tile(r, k), diag_tile(k)).astype(bf16)
                left[tile_at(r, k)] = dot(diag_tile(r), lin[tile_at(r, k)]).astype(bf16)
    for n in range(groups):
        for r in range(groups):
            inside = r < owned and n < owned
            out = own_product[tile_at(r, n)] if inside else None
            for k in range(groups):
                if near(r, k, groups) and near(k, n, groups) and not (inside and k < owned):
                    part = dot(left_tile(r, k), lin_tile(k, n))
                    out = part if out is None else out + part
            if out is None:
                out = jnp.zeros((span, span), f32)
            if near(r, n, groups):
                out = out - left_tile(r, n).astype(f32)
            if r == n:
                out = out + diag_tile(r).astype(f32)
            phi[tile_at(r, n)] = out.astype(bf16)


def advance(parts, full, force, far_force, iterates, images):
    own, ens = force.shape
    mine = full[:own, :ens] + force.astype(f32)
    iterates[0] = mine
    moved = full[:, ens:].astype(bf16)
    images[0] = moved[:own]
    rows = [mine.astype(bf16)]
    for p in range(parts - 1):
        far = full[own * (p + 1):own * (p + 2), :ens]
        if far_force is not None:
            far = far + far_force[p].astype(f32)
        rows.append(far.astype(bf16))
    return jnp.concatenate([jnp.concatenate(rows, axis=0), moved], axis=1)


def opening_kernel(parts, phi, tall, first, *refs):
    far_first, out = refs[:parts - 1], refs[parts - 1]
    begin = jnp.concatenate([first[...]] + [r[...] for r in far_first], axis=0)
    size = tall.shape[1] // 2
    out[...] = dot(phi[...], jnp.concatenate([begin, tall[:, :size]], axis=1))


def early_kernel(parts, i, phi, state, force, *refs):
    far_force = refs[:parts - 1]
    iterates, images, out = refs[parts - 1:]
    own, ens = iterates.shape[1:]
    far = [r[i].reshape(own, ens) for r in far_force]
    current = advance(parts, state[...], force[i].reshape(own, ens), far, iterates, images)
    out[...] = dot(phi[...], current)


def ahead_kernel(phi, both, late, extra, out, cross):
    size = both.shape[0]
    own = late.shape[0]
    count = extra.shape[0] - Q
    table = dot(both[...], phi[...]).astype(bf16)
    out[...] = table
    share = dot(table[:, :own], late[...])
    share = share + jnp.concatenate(
        [extra[:count, :].astype(f32), jnp.zeros((size - count, late.shape[1]), f32)], axis=0
    )
    cross[:size, :] = share.astype(bf16)
    cross[size:, :] = extra[count:, :]


def approach_kernel(parts, state, ahead, late, extra, iterates, images, partial, coarse_phi):
    _, ens = iterates.shape[1:]
    size = partial.shape[0]
    count = extra.shape[0] - Q
    current = advance(parts, state[...], late[...], None, iterates, images)
    got = dot(ahead[...], current)
    partial[...] = got[:, :ens] + jnp.concatenate(
        [extra[:count, :].astype(f32), jnp.zeros((size - count, ens), f32)], axis=0
    )
    coarse_phi[...] = got[:, ens:]


def late_kernel(parts, partial, gram, *refs):
    far_cross = refs[:parts - 1]
    start, sent = refs[parts - 1:]
    size = partial.shape[0]
    each = size // parts
    begin = partial[...]
    for p, r in enumerate(far_cross):
        turn = size - each * (p + 1)
        begin = begin + jnp.concatenate(
            [r[turn:size, :].astype(f32), r[:turn, :].astype(f32)], axis=0
        )
    part = begin.astype(bf16)
    high, low = high_low(gram[...])
    start[:size, :] = begin
    start[size:, :] = begin - (dot(high, part) + dot(low, part))
    sent[...] = part


def defect_kernel(parts, phi, state, last, force, *refs):
    far_late = refs[:parts - 1]
    iterates, images = refs[parts - 1:]
    own, ens = force.shape
    full = state[...]
    rows = [last[0]] + [
        full[own * (p + 1):own * (p + 2), :ens] + r[:own, :].astype(f32)
        for p, r in enumerate(far_late)
    ]
    current = jnp.concatenate([jnp.concatenate(rows, axis=0), full[:, ens:]], axis=1).astype(bf16)
    full = dot(phi[:own, :], current)
    iterates[0] = full[:, :ens] + force[...].astype(f32)
    images[0] = full[:, ens:].astype(bf16)


def write_powers(out, step, moved):
    wide = step.shape[0]
    for at, value in enumerate((step, moved)):
        high, low = high_low(value)
        out[pl.ds(at * wide, wide), :wide] = high
        out[pl.ds(at * wide, wide), wide:] = low


def bit_of_place(i):
    return lax.rem(lax.shift_right_logical(lax.axis_index("tm"), i), 2) == 1


def recurrence_kernel(gram, own_coarse, *refs):
    far_cross = refs[:-5]
    coarse_phi, step_out, out, table, held = refs[-5:]
    size = coarse_phi.shape[0]
    each = own_coarse.shape[0]
    lane = lax.broadcasted_iota(jnp.int32, (Q, size), 1)
    row = lax.broadcasted_iota(jnp.int32, (Q, size), 0)
    pick = (lane % Q == row).astype(f32)
    spread = [dot_f32(own_coarse[...], pick)]
    for r in far_cross:
        pair = r[pl.ds(size, Q), :].astype(f32)
        spread.append(lax.dot_general(
            pair[:, :each] + pair[:, each:2 * each], pick, (((0,), (0,)), ((), ())),
            preferred_element_type=f32, precision=highest,
        ))
    same = (
        lax.broadcasted_iota(jnp.int32, (size, size), 0) // Q
        == lax.broadcasted_iota(jnp.int32, (size, size), 1) // Q
    )
    a = jnp.where(same, jnp.concatenate(spread, axis=0), 0.0)
    lower = coarse_phi[...] - dot_split(gram[...], a)
    step = jnp.concatenate(
        [
            jnp.concatenate([a, jnp.zeros((size, size), f32)], axis=1),
            jnp.concatenate([lower, a], axis=1),
        ],
        axis=0,
    )
    step_out[...] = step
    wide = 2 * size
    high, low = high_low(step)
    out[:, :wide] = high
    out[:, wide:] = low
    ahead = jnp.concatenate([unit(size), unit(size) - gram[...]], axis=0)
    for k in range(4):
        held[k] = ahead.astype(bf16)
        if k < 3:
            ahead = dot_split(step, ahead)
    held[4] = jnp.zeros_like(held[4])
    mine = lax.rem(lax.axis_index("tm"), 4)
    for d in range(4):
        theirs = lax.bitwise_xor(mine, d)
        passed = mine - 1 - theirs
        for top, at in ((0, 3 - theirs), (wide, jnp.where(passed >= 0, passed, 4))):
            table[pl.ds(top, wide), pl.ds(d * size, size)] = held[at]


def powers_kernel(bits, step_in, *outs):
    step = step_in[...]
    moved = unit(step.shape[0])
    for i in range(bits):
        upper = bit_of_place(i)
        if i >= 2:
            write_powers(outs[i - 2], step, jnp.where(upper, moved, 0.0))
        if i < bits - 1:
            moved = jnp.where(upper, step if i == 0 else dot_split(moved, step), moved)
        if i < bits - 2:
            step = dot_split(step, step)


def plane_kernel(table, *refs):
    parts, (total, prefix) = refs[:-2], refs[-2:]
    came = jnp.concatenate([r[...] for r in parts], axis=0)
    moved = dot(table[...], came)
    wide = prefix.shape[0]
    total[...] = moved[:wide].astype(bf16)
    prefix[...] = moved[wide:]


def join_kernel(turn, powers, mine, other, before, total, prefix):
    wide = mine.shape[0]
    upper = bit_of_place(turn)
    own, came = mine[...].astype(f32), other[...].astype(f32)
    low = jnp.where(upper, came, own).astype(bf16)
    high = jnp.where(upper, own, came)
    moved = dot(powers[:, :wide], low)
    total[...] = (moved[:wide] + high).astype(bf16)
    prefix[...] = before[...] + moved[wide:]


def map_kernel(powers, step, tall, *refs):
    images, out = refs[:-1], refs[-1]
    own = out.shape[1]
    wide = powers.shape[0] // 2
    size = wide // 2
    shift = powers[pl.ds(wide, wide), :wide].astype(f32) + powers[pl.ds(wide, wide), wide:].astype(f32)
    high, low = high_low(shift)
    table = step[pl.ds(0, wide), :]
    ahead = dot(table, jnp.concatenate([high, high], axis=0)) + dot(table[:, :wide], low)
    came = (shift[:size] + shift[size:]).astype(bf16)
    at = 0
    for image in images:
        for i in range(image.shape[0]):
            if at < STEPS - 1:
                out[at] = dot(image[i], came).astype(bf16)
            else:
                last = dot(image[i], high[:size])
            at += 1
    m = tall[:own, :]
    both = (ahead[:size] + ahead[size:]).astype(bf16)
    first = ahead[:size].astype(bf16)
    out[STEPS - 1] = dot(m, jnp.concatenate([both, both], axis=0)).astype(bf16)
    out[STEPS] = (last - dot(m, jnp.concatenate([first, first], axis=0))).astype(bf16)


def base_kernel(before, step, start, tall, *refs):
    pairs, base = refs[:-1], refs[-1]
    own = base.shape[1]
    wide = before.shape[0]
    size = wide // 2
    prefix = before[...]
    low = prefix.astype(bf16)
    sum_low = (prefix[:size] + prefix[size:]).astype(bf16)
    mine = dot(step[pl.ds(0, wide), :], jnp.concatenate([low, low], axis=0)) + start[...]
    first = mine[:size].astype(bf16)
    both = (mine[:size] + mine[size:]).astype(bf16)
    m = tall[:own, :]
    at = 0
    for iterates, images in zip(pairs[::2], pairs[1::2]):
        for i in range(iterates.shape[0]):
            if at < STEPS - 1:
                base[at] = iterates[i] + dot(images[i], sum_low)
            else:
                base[STEPS] = (
                    iterates[i]
                    + dot(images[i], low[:size])
                    - dot(m, jnp.concatenate([first, first], axis=0))
                )
            at += 1
    base[STEPS - 1] = dot(m, jnp.concatenate([both, both], axis=0))


def last_kernel(other, table, base, solution, defect, held, sems):
    came = other[...]
    copies = []
    here = defect.shape[0]
    pieces = sems.shape[1]
    each = here // pieces
    for i in range(STEPS + 1):
        to = solution.at[i] if i < STEPS else defect
        for p in range(pieces):
            rows = pl.ds(p * each * BRICK, each * BRICK)
            bricks = pl.ds(p * each, each)
            value = base[i, rows, :] + dot(table[i, rows, :], came)
            held[i, bricks] = value.reshape((each,) + defect.shape[1:])
            copies.append(
                pltpu.make_async_copy(held.at[i, bricks], to.at[bricks], sems.at[i, p])
            )
            copies[-1].start()
    for copy in copies:
        copy.wait()


def dense_body(initial, forcing, brick_blocks, neighbours, coarse_modes, coarse_blocks):
    here, _, ens = initial.shape
    parts = lax.axis_size("space")
    bricks = here * parts
    own = here * BRICK
    rows = bricks * BRICK
    size = bricks * Q
    slices = lax.axis_size("tm")
    bits = slices.bit_length() - 1
    sds = jax.ShapeDtypeStruct

    def in_hbm(value):
        return pltpu.with_memory_space_constraint(value, pltpu.HBM)

    def others(value):
        return [
            lax.ppermute(value, "space", [((s + k) % parts, s) for s in range(parts)])
            for k in range(1, parts)
        ]

    def paired(value, bit):
        return lax.ppermute(value, "tm", [(j, j ^ (1 << bit)) for j in range(slices)])

    half = here // 2
    coarse = coarse_blocks.reshape(here * Q, Q)
    slots = neighbours.shape[1]
    top = half * (slots + 1) // 2 * BRICK
    some = call(
        half_kernel,
        sds((top + here, 128), bf16),
        [HBM, HBM],
        in_hbm(brick_blocks), in_hbm(neighbours),
        scratch=[
            pltpu.VMEM((half,) + brick_blocks.shape[1:], bf16),
            pltpu.VMEM(neighbours.shape, jnp.int32),
            pltpu.SemaphoreType.DMA((2,)),
        ],
    )
    fetched = others(some)
    start_half, first, send_force = call(
        pack_kernel,
        (sds((own, ens), bf16), sds((own, ens), bf16), sds((STEPS - 2,) + forcing.shape[1:], bf16)),
        [HBM] * 2,
        in_hbm(initial), in_hbm(forcing),
        scratch=[pltpu.VMEM(initial.shape, f32), pltpu.SemaphoreType.DMA((2,))],
    )
    far_first = [
        lax.ppermute(
            start_half, ("tm", "space"), [((s + k) % parts, s) for s in range(parts)]
        )
        for k in range(1, parts)
    ]
    far_force = others(send_force)
    tall, both, extra, late, own_off, own_diag, gram, last_force, own_coarse = call(
        prepare_kernel,
        (
            sds((rows, 2 * size), bf16),
            sds((size, rows), bf16),
            sds((here * Q + Q, ens), bf16),
            sds((own, ens), bf16),
            sds((rows // 128, own, 128), bf16),
            sds((own, GROUP * BRICK), bf16),
            sds((size, size), f32),
            sds((own, ens), bf16),
            sds(coarse.shape, f32),
        ),
        [HBM] * 5,
        in_hbm(neighbours), in_hbm(coarse_modes), in_hbm(coarse), in_hbm(forcing), in_hbm(brick_blocks),
        scratch=[
            pltpu.VMEM((2,) + forcing.shape[1:], bf16),
            pltpu.VMEM(brick_blocks.shape, bf16),
            pltpu.VMEM(coarse_modes.shape, f32),
            pltpu.SMEM(neighbours.shape, jnp.int32),
            pltpu.VMEM((2, BRICK, 128), bf16),
            pltpu.SemaphoreType.DMA((5,)),
        ],
    )
    pieces = [piece for f in fetched for piece in (f, paired(f, 0))]
    far_nbr = [f[top:top + here, :slots].astype(jnp.int32) for f in fetched]
    far_nbr = far_nbr[0] if parts == 2 else jnp.concatenate(far_nbr, axis=0)
    part = call(
        functools.partial(first_kernel, parts),
        (sds((rows // 128, half * BRICK, 128), bf16),) * (parts - 1)
        + (sds((half * BRICK, GROUP * BRICK), bf16),) * (parts - 1)
        + (sds((own, own), bf16), sds((own, own), bf16), sds((own, own), f32)),
        [SMEM] + [VMEM] * (1 + parts),
        far_nbr, own_off, own_diag, *fetched,
        scratch=[pltpu.VMEM((2, BRICK, 128), bf16)],
        flops=2 * 16 * (GROUP * BRICK) ** 3,
    )
    offs, diags = part[:parts - 1], part[parts - 1:2 * parts - 2]
    phi = call(
        functools.partial(operator_kernel, parts),
        sds((rows, rows), bf16),
        [SMEM] + [VMEM] * (2 + 3 * parts),
        far_nbr, own_off, own_diag, *part[2 * parts - 2:], *pieces[1::2], *offs, *diags,
        scratch=[
            pltpu.VMEM((rows // 128, rows - own, 128), bf16),
            pltpu.VMEM((rows - own, GROUP * BRICK), bf16),
            pltpu.VMEM((rows, rows), bf16),
            pltpu.VMEM((rows, rows), bf16),
            pltpu.VMEM((2, BRICK, 128), bf16),
        ],
        flops=2 * 4 * rows * rows * ens,
        vmem=20,
    )
    ahead, cross = call(
        ahead_kernel,
        (sds((size, rows), bf16), sds((size + Q, ens), bf16)),
        [VMEM] * 4,
        phi, both, late, extra,
        flops=2 * size * rows * rows,
    )
    far_cross = others(cross)
    far_late = others(late)
    state = call(
        functools.partial(opening_kernel, parts),
        sds((rows, ens + size), f32),
        [VMEM] * (2 + parts),
        phi, tall, first, *far_first,
        flops=2 * rows * rows * (ens + size),
    )
    early = []
    for i in range(STEPS - 2):
        *pair, state = call(
            functools.partial(early_kernel, parts, i),
            (
                sds((1, own, ens), f32),
                sds((1, own, size), bf16),
                sds((rows, ens + size), f32),
            ),
            [VMEM] * (2 + parts),
            phi, state, send_force, *far_force,
            flops=2 * rows * rows * (ens + size),
        )
        early.append(pair)
    *pair, partial, coarse_phi = call(
        functools.partial(approach_kernel, parts),
        (
            sds((1, own, ens), f32),
            sds((1, own, size), bf16),
            sds((size, ens), f32),
            sds((size, size), f32),
        ),
        [VMEM] * 4,
        state, ahead, late, extra,
        flops=4 * size * rows * (ens + size),
    )
    early.append(pair)
    start, sent = call(
        functools.partial(late_kernel, parts),
        (sds((2 * size, ens), f32), sds((size, ens), bf16)),
        [VMEM] * (1 + parts),
        partial, gram, *far_cross,
        flops=4 * size * own * ens,
    )
    early.append(call(
        functools.partial(defect_kernel, parts),
        (sds((1, own, ens), f32), sds((1, own, size), bf16)),
        [VMEM] * (3 + parts),
        phi, state, pair[0], last_force, *far_late,
        flops=2 * own * rows * (ens + size),
    ))
    table = sds((4 * size, 4 * size), bf16)
    near = []
    for d in range(1, 4):
        near.append(lax.ppermute(sent, "tm", [(j, j ^ d) for j in range(slices)]))
    step, once, plane = call(
        recurrence_kernel,
        (
            sds((2 * size, 2 * size), f32),
            sds((2 * size, 4 * size), bf16),
            sds((4 * size, 4 * size), bf16),
        ),
        [VMEM] * (2 + parts),
        gram, own_coarse, *far_cross, coarse_phi,
        scratch=[pltpu.VMEM((5, 2 * size, size), bf16)],
        flops=2 * 6 * (2 * size) ** 3,
    )
    total, prefix = call(
        plane_kernel,
        (sds((2 * size, ens), bf16), sds((2 * size, ens), f32)),
        [VMEM] * 5,
        plane, sent, *near,
    )
    powers = call(
        functools.partial(powers_kernel, bits),
        (table,) * (bits - 2),
        [VMEM],
        step,
        flops=2 * 18 * (2 * size) ** 3,
    )
    for i in range(2, bits):
        other = paired(total, i)
        if i < bits - 1:
            total, prefix = call(
                functools.partial(join_kernel, i),
                (sds((2 * size, ens), bf16), sds((2 * size, ens), f32)),
                [VMEM] * 4,
                powers[i - 2], total, other, prefix,
            )
    pairs = [ref for pair in early for ref in pair]
    table = call(
        map_kernel,
        sds((STEPS + 1, own, 2 * size), bf16),
        [VMEM] * (3 + len(early)),
        powers[bits - 3], once, tall, *pairs[1::2],
        flops=2 * (STEPS + 2) * own * 2 * size * 2 * size,
    )
    base = call(
        base_kernel,
        sds((STEPS + 1, own, ens), f32),
        [VMEM] * (4 + len(pairs)),
        prefix, once, start, tall, *pairs,
        flops=2 * (STEPS + 1) * own * 2 * size * ens,
    )
    solution_out, defect = call(
        last_kernel,
        (sds((STEPS, here, BRICK, ens), f32), sds((here, BRICK, ens), f32)),
        [VMEM] * 3,
        other, table, base,
        scratch=[
            pltpu.VMEM((STEPS + 1, here, BRICK, ens), f32),
            pltpu.SemaphoreType.DMA((STEPS + 1, 2)),
        ],
        out_space=pl.BlockSpec(memory_space=pl.ANY),
    )
    return solution_out, defect[None]


def solution(mesh):
    placed = (
        P("space", None, None),
        P("tm", "space", None, None),
        P("space", None, None),
        P("space", None),
        P(),
        P("space", None, None),
    )

    def body(initial, *rest):
        here = initial.shape[0]
        bricks = here * lax.axis_size("space")
        slices = lax.axis_size("tm")
        fits = 8 * (bricks * BRICK) ** 2 <= 16 * 2 ** 20
        even = here % (2 * GROUP) == 0 and slices > 4 and slices & (slices - 1) == 0
        even = even and 2 * here * Q == initial.shape[2]
        return (dense_body if fits and even else banded_body)(initial, *rest)

    return jax.shard_map(
        body,
        mesh=mesh,
        in_specs=placed,
        out_specs=(P("tm", "space", None, None), P("tm", "space", None, None)),
        check_vma=False,
    )
```
